256 devices in a mesh: seq: 64 (over z, y, core), head: 2 (over x_lo), sample: 2 (over x_hi).
Axes of the slice: x: 4 (x_hi: 2, x_lo: 2; x = x_hi * 2 + x_lo), y: 4, z: 8, core: 2. Of those that a mesh axis runs over, the one named last changes fastest.
Arguments:
- features: bfloat16 [2, 16384, 1536], P('sample', 'seq'), may hold values from -16 to 16
- dilated_weight: bfloat16 [1536, 3, 768], P(None, None, 'head'), may hold values from -0.09375 to 0.09375
- point_weight: bfloat16 [1536, 768], P(None, 'head'), may hold values from -0.21875 to 0.21875
- track_weight: bfloat16 [1536, 3840], P('sample', 'head'), may hold values from -0.15625 to 0.15625
- track_cotangent: bfloat16 [2, 16384, 3840], P('sample', 'seq', 'head'), may hold values from -6 to 6
Outputs:
- input_grad: bfloat16 [2, 16384, 1536], P('sample', 'seq')
- dilated_grad: float32 [1536, 3, 768], P(('seq', 'sample'), None, 'head')
- point_grad: float32 [1536, 768], P(('seq', 'sample'), 'head')
The draws below stay inside these ranges and needn't reach their ends.
All inputs are finite; a program needn't handle non-finite values.
Results may differ from the reference program's by a relative error of at most 0.015.
Values may be sent and summed in bfloat16 or wider, within the bound.
A program may use at most 128 MiB of HBM per device.

```python
import jax
import jax.numpy as jnp
from jax import lax

C = 1536
F = 768
TRACKS = 3840
DILATION_STEP = 1024
L = 16384
BATCH = 2
N_HEAD = 2


def spiked(drawn, key, source, target, blocks, factor):
    def block_of(axis_at):
        return (jnp.arange(drawn.shape[axis_at]) // (drawn.shape[axis_at] // blocks)).reshape((-1,) + (1,) * (drawn.ndim - 1 - axis_at))

    one_side = jax.random.permutation(key, blocks)[block_of(target)]
    far = (block_of(target) + blocks // 2) % blocks
    return jnp.where((block_of(source) == one_side) | (block_of(source) == far), factor * drawn, drawn)


def block_levels(stream_key, extent, split, smallest, top_value):
    def one(axis_at, blocks):
        heights = jax.random.uniform(jax.random.fold_in(jax.random.fold_in(stream_key, 6), axis_at), (blocks,), jnp.float32, smallest / len(split), top_value / len(split))
        return jnp.repeat(jnp.exp(heights), extent[axis_at] // blocks).reshape((-1,) + (1,) * (len(extent) - axis_at - 1))

    gain = one(*split[0])
    for cut in split[1:]:
        gain = gain * one(*cut)
    return gain


def noise(rng, shape, spread, most, cuts=(), kind=jnp.bfloat16):
    drawn = spread * jax.random.normal(rng, shape, jnp.float32)
    if cuts:
        drawn = drawn * block_levels(rng, shape, cuts, -0.22, 0.18)
    return jnp.clip(drawn, -most, most).astype(kind)


def gaussian_with(key, extent, width, reach, cuts, heavy, kind=jnp.bfloat16):
    entries = width * jax.random.normal(key, extent, jnp.float32)
    if cuts:
        entries = entries * block_levels(key, extent, cuts, -0.22, 0.18)
    return jnp.clip(spiked(entries, jax.random.fold_in(key, 3), *heavy), -reach, reach).astype(kind)


def setup_inputs(seed: int = 0) -> dict:
    seeds = jax.random.split(jax.random.key(seed), 6)
    return {
        "features": gaussian_with(seeds[0], (BATCH, L, C), 1.0, 16.0, ((0, 2), (1, 64)), (1, 2, 64, 4.0)),
        "dilated_weight": noise(seeds[1], (C, 3, F), (3 * C) ** -0.5, 0.09375, ((2, 2),)),
        "point_weight": noise(seeds[2], (C, F), F ** -0.5, 0.21875, ((1, 2),)),
        "track_weight": noise(seeds[3], (C, TRACKS), C ** -0.5, 0.15625, ((0, 2), (1, 2))),
        "track_cotangent": noise(seeds[4], (BATCH, L, TRACKS), 1.0, 6.0, ((0, 2), (1, 64), (2, 2))),
    }


def gelu_value(value):
    inner = 0.7978845608 * (value + 0.044715 * value * value * value)
    return 0.5 * value * (1.0 + jnp.tanh(inner))


def gelu_slope(value):
    inner = 0.7978845608 * (value + 0.044715 * value * value * value)
    tangent = jnp.tanh(inner)
    return 0.5 * (1.0 + tangent) + 0.5 * value * (1.0 - tangent * tangent) * 0.7978845608 * (1.0 + 3.0 * 0.044715 * value * value)


def shifted_input(field, amount):
    empty = jnp.zeros((abs(amount),) + field.shape[1:], field.dtype)
    if amount > 0:
        return jnp.concatenate([empty, field[:-amount]], axis=0)
    return jnp.concatenate([field[-amount:], empty], axis=0)


def rounded(value):
    return lax.optimization_barrier(value.astype(jnp.bfloat16)).astype(jnp.float32)


def one_sample(features, track_cotangent, dilated_weight, point_weight, track_weight):
    feat_wide = features.astype(jnp.float32)
    activated_hidden = gelu_value(feat_wide).astype(jnp.bfloat16)
    preceding_value = shifted_input(activated_hidden, DILATION_STEP)
    following_value = shifted_input(activated_hidden, -DILATION_STEP)
    middle = jnp.dot(preceding_value, dilated_weight[:, 0, :], preferred_element_type=jnp.float32)
    middle = middle + jnp.dot(activated_hidden, dilated_weight[:, 1, :], preferred_element_type=jnp.float32)
    middle = middle + jnp.dot(following_value, dilated_weight[:, 2, :], preferred_element_type=jnp.float32)
    hidden = gelu_value(middle).astype(jnp.bfloat16)
    group_width = F // N_HEAD
    track_width = TRACKS // N_HEAD
    summed = feat_wide
    for group in range(N_HEAD):
        lower = group * group_width
        part = jnp.dot(hidden[:, lower:lower + group_width], point_weight[:, lower:lower + group_width].T, preferred_element_type=jnp.float32)
        summed = summed + rounded(part)
    block_out = summed.astype(jnp.bfloat16)
    scores = jnp.dot(block_out, track_weight, preferred_element_type=jnp.float32)
    score_grad = (track_cotangent.astype(jnp.float32) * jax.nn.sigmoid(scores)).astype(jnp.bfloat16)
    out_grad = jnp.zeros(feat_wide.shape, jnp.float32)
    for group in range(N_HEAD):
        lower = group * track_width
        part = jnp.dot(score_grad[:, lower:lower + track_width], track_weight[:, lower:lower + track_width].T, preferred_element_type=jnp.float32)
        out_grad = out_grad + rounded(part)
    out_grad_b = out_grad.astype(jnp.bfloat16)
    hidden_grad = jnp.dot(out_grad_b, point_weight, preferred_element_type=jnp.float32)
    middle_gradient = (hidden_grad * gelu_slope(middle)).astype(jnp.bfloat16)
    kernel_taps = jnp.stack([shifted_input(middle_gradient, -DILATION_STEP), middle_gradient, shifted_input(middle_gradient, DILATION_STEP)], axis=1)
    positions = kernel_taps.shape[0]
    dilated_grad = jnp.dot(activated_hidden.T, kernel_taps.reshape(positions, 3 * F), preferred_element_type=jnp.float32).reshape(C, 3, F)
    point_grad = jnp.dot(out_grad_b.T, hidden, preferred_element_type=jnp.float32)
    act_grad = jnp.zeros(feat_wide.shape, jnp.float32)
    for group in range(N_HEAD):
        lower = group * group_width
        tap_group = kernel_taps[:, :, lower:lower + group_width].reshape(positions, 3 * group_width)
        weight_group = dilated_weight[:, :, lower:lower + group_width].reshape(C, 3 * group_width)
        act_grad = act_grad + rounded(jnp.dot(tap_group, weight_group.T, preferred_element_type=jnp.float32))
    input_grad = (out_grad + act_grad * gelu_slope(feat_wide)).astype(jnp.bfloat16)
    return input_grad, dilated_grad, point_grad


def reference(features, dilated_weight, point_weight, track_weight, track_cotangent):
    def single(pair):
        return one_sample(pair[0], pair[1], dilated_weight, point_weight, track_weight)

    input_grad, dilated_grad, point_grad = lax.map(single, (features, track_cotangent))
    return input_grad, jnp.sum(dilated_grad, axis=0), jnp.sum(point_grad, axis=0)
```

```python
import jax
import jax.numpy as jnp
from jax import lax
from jax.experimental import pallas as pl
from jax.experimental.pallas import tpu as pltpu
from jax.sharding import Mesh
from jax.sharding import PartitionSpec as P

MESH = pl.DeviceIdType.MESH
SEQ = ("z", "y", "c")
SEQ_SAMPLE = ("z", "y", "c", "s")
NZ, NY = 8, 4
YROWS, ZROWS = 64, 16
SUBS = 4
VMEM = pl.BlockSpec(memory_space=pltpu.VMEM)
ANY = pl.BlockSpec(memory_space=pl.ANY)
DMA = pltpu.SemaphoreType.DMA


def gelu_value(value):
    inner = 0.7978845608 * (value + 0.044715 * value * value * value)
    return 0.5 * value * (1.0 + jnp.tanh(inner))


def gelu_slope(value):
    inner = 0.7978845608 * (value + 0.044715 * value * value * value)
    tangent = jnp.tanh(inner)
    return 0.5 * (1.0 + tangent) + 0.5 * value * (1.0 - tangent * tangent) * 0.7978845608 * (
        1.0 + 3.0 * 0.044715 * value * value
    )


def times(left, right):
    return jnp.dot(left, right, preferred_element_type=jnp.float32)


def times_transposed(left, right):
    return lax.dot_general(
        left, right, (((1,), (1,)), ((), ())), preferred_element_type=jnp.float32
    )


def transposed_times(left, right):
    return lax.dot_general(
        left, right, (((0,), (0,)), ((), ())), preferred_element_type=jnp.float32
    )


def place():
    return tuple(lax.axis_index(name) for name in ("z", "y", "c", "h", "s"))


def remote(source, target, sent, arrived, **device):
    return pltpu.make_async_remote_copy(
        src_ref=source,
        dst_ref=target,
        send_sem=sent,
        recv_sem=arrived,
        device_id=device,
        device_id_type=MESH,
    )


def greet(barrier, **device):
    pl.semaphore_signal(barrier, inc=1, device_id=device, device_id_type=MESH)


def rows_at(start, size):
    return pl.ds(pl.multiple_of(start, 16), size)


def shifted(z, y, step):
    at = z * NY + y + step
    return {"z": lax.div(at, NY), "y": lax.rem(at, NY)}


def has_neighbours(z, y):
    at = z * NY + y
    return at >= 2, at < NZ * NY - 2


def send_halo(z, y, ahead, behind, sent, arrived):
    before, after = has_neighbours(z, y)

    @pl.when(after)
    def _():
        remote(*ahead, sent.at[0], arrived.at[0], **shifted(z, y, 2)).start()

    @pl.when(before)
    def _():
        remote(*behind, sent.at[1], arrived.at[1], **shifted(z, y, -2)).start()


def wait_halo(z, y, ahead, behind, sent, arrived):
    before, after = has_neighbours(z, y)

    @pl.when(before)
    def _():
        remote(*ahead, sent.at[0], arrived.at[0], c=lax.axis_index("c")).wait_recv()

    @pl.when(jnp.logical_not(before))
    def _():
        ahead[1][...] = jnp.zeros_like(ahead[1])

    @pl.when(after)
    def _():
        remote(*behind, sent.at[1], arrived.at[1], c=lax.axis_index("c")).wait_recv()

    @pl.when(jnp.logical_not(after))
    def _():
        behind[1][...] = jnp.zeros_like(behind[1])


def drain_halo(z, y, ahead, behind, sent, arrived):
    before, after = has_neighbours(z, y)

    @pl.when(after)
    def _():
        remote(*ahead, sent.at[0], arrived.at[0], c=lax.axis_index("c")).wait_send()

    @pl.when(before)
    def _():
        remote(*behind, sent.at[1], arrived.at[1], c=lax.axis_index("c")).wait_send()


def greet_halo(barrier, z, y):
    before, after = has_neighbours(z, y)

    @pl.when(after)
    def _():
        greet(barrier, **shifted(z, y, 2))

    @pl.when(before)
    def _():
        greet(barrier, **shifted(z, y, -2))

    return before.astype(jnp.int32) + after.astype(jnp.int32)


def forward_kernel(
    q0, q2, centre, tw, pw, middle, hidden, twf, pwo,
    from_before, from_after, own, own_sem,
    halo_s, halo_r, hid_s, hid_r, x_s, x_r, y_s, y_r, tz_s, tz_r, pz_s, pz_r, sib_s, sib_r,
):
    z, y, c, h, s = place()
    up, down = lax.rem(z + 1, NZ), lax.rem(z + NZ - 1, NZ)
    barrier = pltpu.get_barrier_semaphore()
    greet(barrier, h=1 - h)
    greet(barrier, s=1 - s)
    greet(barrier, c=1 - c)
    greet(barrier, z=up)
    greet(barrier, z=down)
    for step in range(1, NY):
        greet(barrier, y=lax.rem(y + step, NY))
    count = greet_halo(barrier, z, y)
    pl.semaphore_wait(barrier, 8 + count)

    half = tw.shape[0] // 2
    pw_rows = pw.shape[0] // 2 // NZ
    base = c * half

    def y_piece(at):
        return rows_at(base + at * YROWS, YROWS)

    def z_piece(at):
        return rows_at(base + NY * YROWS + at * ZROWS, ZROWS)

    def p_piece(at):
        return rows_at(c * (pw.shape[0] // 2) + at * pw_rows, pw_rows)

    ahead, behind = (q0, from_before), (q2, from_after)
    send_halo(z, y, ahead, behind, halo_s, halo_r)
    to_sample = [
        remote(tw.at[z_piece(z)], twf.at[s, z_piece(z)], x_s.at[0], x_r.at[0], s=1 - s),
        remote(tw.at[y_piece(y)], twf.at[s, y_piece(y)], x_s.at[1], x_r.at[1], s=1 - s),
    ]
    to_head = remote(pw.at[p_piece(z)], pwo.at[p_piece(z)], x_s.at[2], x_r.at[2], h=1 - h)
    to_sample[0].start()
    to_head.start()
    to_sample[1].start()
    take_own = pltpu.make_async_copy(tw, own, own_sem.at[0])
    take_own.start()

    started = [*to_sample, to_head]
    landed = []
    other = 1 - s

    def track_sibling(rows, slot):
        copy = remote(twf.at[other, rows], twf.at[other, rows], sib_s.at[slot], sib_r.at[slot], c=1 - c)
        copy.start()
        started.append(copy)

    def point_sibling(rows, slot):
        copy = remote(pwo.at[rows], pwo.at[rows], sib_s.at[slot], sib_r.at[slot], c=1 - c)
        copy.start()
        started.append(copy)

    def send_z(at, slot, target):
        rows = z_piece(at)
        copy = remote(twf.at[other, rows], twf.at[other, rows], tz_s.at[slot], tz_r.at[slot], z=target)
        copy.start()
        started.append(copy)

    def send_p(at, slot, target):
        rows = p_piece(at)
        copy = remote(pwo.at[rows], pwo.at[rows], pz_s.at[slot], pz_r.at[slot], z=target)
        copy.start()
        started.append(copy)

    to_sample[0].wait_recv()
    send_z(z, 0, up)
    send_z(z, 4, down)
    to_head.wait_recv()
    send_p(z, 0, up)
    send_p(z, 4, down)
    track_sibling(z_piece(z), 0)
    point_sibling(p_piece(z), 8)

    take_own.wait()
    put_own = pltpu.make_async_copy(own, twf.at[s], own_sem.at[1])
    put_own.start()

    def ring_step(step):
        for send, sem_s, sem_r, buf, piece, slot, sibling, first in (
            (send_z, tz_s, tz_r, None, z_piece, 0, track_sibling, 0),
            (send_p, pz_s, pz_r, pwo, p_piece, 0, point_sibling, 8),
        ):
            ref = twf.at[other] if buf is None else buf
            at = lax.rem(z + NZ - step, NZ)
            remote(ref.at[piece(at)], ref.at[piece(at)], sem_s.at[step - 1], sem_r.at[step - 1], z=up).wait_recv()
            if step < 4:
                send(at, step, up)
            sibling(piece(at), first + step)
            if step < 4:
                at = lax.rem(z + step, NZ)
                remote(ref.at[piece(at)], ref.at[piece(at)], sem_s.at[step + 3], sem_r.at[step + 3], z=up).wait_recv()
                if step < 3:
                    send(at, 4 + step, down)
                sibling(piece(at), first + 4 + step)

    ring_step(1)
    to_sample[1].wait_recv()
    rows = y_piece(y)
    for step in range(1, NY):
        copy = remote(
            twf.at[other, rows], twf.at[other, rows], y_s.at[step - 1], y_r.at[step - 1],
            y=lax.rem(y + step, NY),
        )
        copy.start()
        started.append(copy)
    track_sibling(rows, 16)
    ring_step(2)

    wait_halo(z, y, ahead, behind, halo_s, halo_r)
    total = centre[...] + from_before[...].astype(jnp.float32) + from_after[...].astype(jnp.float32)
    middle[...] = total
    hidden[0] = gelu_value(total).astype(jnp.bfloat16)
    to_partner = remote(hidden.at[0], hidden.at[1], hid_s, hid_r, h=1 - h)
    to_partner.start()
    started.append(to_partner)
    ring_step(3)
    ring_step(4)
    for step in range(1, NY):
        rows = y_piece(lax.rem(y + NY - step, NY))
        remote(
            twf.at[other, rows], twf.at[other, rows], y_s.at[step - 1], y_r.at[step - 1], y=y
        ).wait_recv()
        track_sibling(rows, 16 + step)
    to_partner.wait_recv()

    sib_base = (1 - c) * half
    sib_point = (1 - c) * (pw.shape[0] // 2)
    for slot in range(20):
        step = slot % 8 if slot < 16 else slot - 16
        if slot < 16:
            at = lax.rem(z + NZ - step, NZ) if step <= 4 else lax.rem(z + step - 4, NZ)
        else:
            at = lax.rem(y + NY - step, NY)
        if slot < 8:
            ref = twf.at[other, rows_at(sib_base + NY * YROWS + at * ZROWS, ZROWS)]
        elif slot < 16:
            ref = pwo.at[rows_at(sib_point + at * pw_rows, pw_rows)]
        else:
            ref = twf.at[other, rows_at(sib_base + at * YROWS, YROWS)]
        remote(ref, ref, sib_s.at[slot], sib_r.at[slot], c=1 - c).wait_recv()
    for copy in started:
        copy.wait_send()
    drain_halo(z, y, ahead, behind, halo_s, halo_r)
    put_own.wait()


def forward_exchange(q0, q2, centre, tw, pw):
    rows, width = q0.shape
    return pl.pallas_call(
        forward_kernel,
        out_shape=(
            jax.ShapeDtypeStruct((rows, width), jnp.float32),
            jax.ShapeDtypeStruct((2, rows, width), jnp.bfloat16),
            jax.ShapeDtypeStruct((2, *tw.shape), jnp.bfloat16),
            jax.ShapeDtypeStruct(pw.shape, jnp.bfloat16),
        ),
        in_specs=[VMEM, VMEM, VMEM, ANY, ANY],
        out_specs=(VMEM, VMEM, ANY, ANY),
        scratch_shapes=[
            pltpu.VMEM((rows, width), jnp.bfloat16),
            pltpu.VMEM((rows, width), jnp.bfloat16),
            pltpu.VMEM(tw.shape, jnp.bfloat16),
            DMA((2,)),
            DMA((2,)), DMA((2,)),
            DMA, DMA,
            DMA((3,)), DMA((3,)),
            DMA((3,)), DMA((3,)),
            DMA((7,)), DMA((7,)),
            DMA((7,)), DMA((7,)),
            DMA((20,)), DMA((20,)),
        ],
        compiler_params=pltpu.CompilerParams(collective_id=0, has_side_effects=True),
        name="forward_exchange",
    )(q0, q2, centre, tw, pw)


def swap_kernel(mine, theirs, sent, arrived):
    h = lax.axis_index("h")
    barrier = pltpu.get_barrier_semaphore()
    greet(barrier, h=1 - h)
    pl.semaphore_wait(barrier, 1)
    copy = remote(mine, theirs, sent, arrived, h=1 - h)
    copy.start()
    copy.wait()


def head_swap(mine):
    return pl.pallas_call(
        swap_kernel,
        out_shape=jax.ShapeDtypeStruct(mine.shape, mine.dtype),
        in_specs=[VMEM],
        out_specs=VMEM,
        scratch_shapes=[DMA, DMA],
        compiler_params=pltpu.CompilerParams(collective_id=1, has_side_effects=True),
        name="head_swap",
    )(mine)


def halo_kernel(grad, later, earlier, sent, arrived):
    z, y, c, h, s = place()
    barrier = pltpu.get_barrier_semaphore()
    count = greet_halo(barrier, z, y)
    pl.semaphore_wait(barrier, count)
    ahead, behind = (grad, earlier), (grad, later)
    send_halo(z, y, ahead, behind, sent, arrived)
    wait_halo(z, y, ahead, behind, sent, arrived)
    drain_halo(z, y, ahead, behind, sent, arrived)


def halo_exchange(grad):
    shape = jax.ShapeDtypeStruct(grad.shape, grad.dtype)
    return pl.pallas_call(
        halo_kernel,
        out_shape=(shape, shape),
        in_specs=[VMEM],
        out_specs=(VMEM, VMEM),
        scratch_shapes=[DMA((2,)), DMA((2,))],
        compiler_params=pltpu.CompilerParams(collective_id=2, has_side_effects=True),
        name="halo_exchange",
    )(grad)


def reduce_kernel(
    grads, act, summed, act_other,
    sibling, sendbuf, recvbuf, final, last_send, last_recv,
    act_s, act_r, sib_s, sib_r, ring_s, ring_r, last_s, last_r,
):
    z, y, c, h, s = place()
    up, down = lax.rem(z + 1, NZ), lax.rem(z + NZ - 1, NZ)
    me = (y * 2 + c) * 2 + s

    def group(at):
        return {"y": lax.div(at, 4), "c": lax.rem(lax.div(at, 2), 2), "s": lax.rem(at, 2)}

    barrier = pltpu.get_barrier_semaphore()
    greet(barrier, c=1 - c)
    greet(barrier, z=up)
    greet(barrier, z=down)
    greet(barrier, h=1 - h)
    for step in range(1, 16):
        greet(barrier, **group(lax.rem(me + step, 16)))
    pl.semaphore_wait(barrier, 19)

    rows = grads.shape[1] // NZ
    width = grads.shape[2] // 2
    sub = rows // SUBS
    act_copy = remote(act, act_other, act_s, act_r, h=1 - h)
    order = (7, 1, 6, 2, 5, 3, 4, 0)
    siblings = []
    for slot, offset in enumerate(order):
        at = rows_at(lax.rem(z + offset, NZ) * rows, rows)
        copy = remote(grads.at[1 - c, at], sibling.at[at], sib_s.at[slot], sib_r.at[slot], c=1 - c)
        copy.start()
        siblings.append(copy)
    act_copy.start()

    def columns(way):
        return pl.ds(way * width, width)

    def partial(at, way, piece):
        where = rows_at(at * rows + piece * sub, sub)
        mine = grads[c, where, columns(way)].astype(jnp.float32)
        return mine + sibling[where, columns(way)].astype(jnp.float32)

    def ring_copy(step, way, piece):
        return remote(
            sendbuf.at[step, way, piece], recvbuf.at[step, way, piece],
            ring_s.at[step, way, piece], ring_r.at[step, way, piece], z=up if way == 0 else down,
        )

    def target(step, way):
        return lax.rem(z + 2 * NZ - 1 - step, NZ) if way == 0 else lax.rem(z + 1 + step, NZ)

    def ring_step(step):
        for piece in range(SUBS):
            for way in range(2):
                value = partial(target(step, way), way, piece)
                ring_copy(step - 1, way, piece).wait_recv()
                value = value + recvbuf[step - 1, way, piece].astype(jnp.float32)
                sendbuf[step, way, piece] = value.astype(jnp.bfloat16)
                ring_copy(step, way, piece).start()

    siblings[0].wait_recv()
    siblings[1].wait_recv()
    for piece in range(SUBS):
        for way in range(2):
            sendbuf[0, way, piece] = partial(target(0, way), way, piece).astype(jnp.bfloat16)
            ring_copy(0, way, piece).start()
    for copy in siblings[2:]:
        copy.wait_recv()

    def body(step, carry):
        ring_step(step)
        return carry

    lax.fori_loop(1, NZ - 1, body, 0)
    for piece in range(SUBS):
        for way in range(2):
            value = partial(z, way, piece)
            ring_copy(NZ - 2, way, piece).wait_recv()
            value = value + recvbuf[NZ - 2, way, piece].astype(jnp.float32)
            final[pl.ds(piece * sub, sub), columns(way)] = value
    each = rows // 16
    for at in range(16):
        last_send[at] = final[at * each:(at + 1) * each, :].astype(jnp.bfloat16)
    lasts = []
    for step in range(1, 16):
        to = lax.rem(me + step, 16)
        copy = remote(
            last_send.at[to], last_recv.at[me], last_s.at[step - 1], last_r.at[step - 1], **group(to)
        )
        copy.start()
        lasts.append(copy)
    last_recv[me] = last_send[me]
    for step in range(1, 16):
        source = lax.rem(me + 16 - step, 16)
        remote(
            last_send.at[source], last_recv.at[source], last_s.at[step - 1], last_r.at[step - 1], c=c
        ).wait_recv()
    for core in range(2):
        total = jnp.zeros((each, 2 * width), jnp.float32)
        for row in range(NY):
            for sample in range(2):
                total = total + last_recv[(row * 2 + core) * 2 + sample].astype(jnp.float32)
        summed[core] = total
    act_copy.wait()
    for copy in siblings:
        copy.wait_send()
    for copy in lasts:
        copy.wait_send()

    def drain(step, carry):
        for piece in range(SUBS):
            for way in range(2):
                ring_copy(step, way, piece).wait_send()
        return carry

    lax.fori_loop(0, NZ - 1, drain, 0)


def reduce_and_swap(grads, act):
    _, channels, width = grads.shape
    rows = channels // NZ
    each = rows // 16
    sub = rows // SUBS
    return pl.pallas_call(
        reduce_kernel,
        out_shape=(
            jax.ShapeDtypeStruct((2, each, width), jnp.float32),
            jax.ShapeDtypeStruct(act.shape, act.dtype),
        ),
        in_specs=[VMEM, VMEM],
        out_specs=(VMEM, VMEM),
        scratch_shapes=[
            pltpu.VMEM((channels, width), jnp.bfloat16),
            pltpu.VMEM((NZ - 1, 2, SUBS, sub, width // 2), jnp.bfloat16),
            pltpu.VMEM((NZ - 1, 2, SUBS, sub, width // 2), jnp.bfloat16),
            pltpu.VMEM((rows, width), jnp.float32),
            pltpu.VMEM((16, each, width), jnp.bfloat16),
            pltpu.VMEM((16, each, width), jnp.bfloat16),
            DMA, DMA,
            DMA((8,)), DMA((8,)),
            DMA((NZ - 1, 2, SUBS)), DMA((NZ - 1, 2, SUBS)),
            DMA((15,)), DMA((15,)),
        ],
        compiler_params=pltpu.CompilerParams(collective_id=3, has_side_effects=True),
        name="reduce_and_swap",
    )(grads, act)


def body(features, dilated_weight, point_weight, track_weight, track_cotangent):
    samples, positions, channels = features.shape
    number_rows = samples * positions
    width = dilated_weight.shape[2]
    feat_wide = features.reshape(number_rows, channels).astype(jnp.float32)
    activated = gelu_value(feat_wide).astype(jnp.bfloat16)
    taps_weight = [dilated_weight[:, tap, :] for tap in range(3)]
    to_later = times(activated, taps_weight[0]).astype(jnp.bfloat16)
    to_earlier = times(activated, taps_weight[2]).astype(jnp.bfloat16)
    centre = times(activated, taps_weight[1])
    middle, hidden, whole_track, other_point = forward_exchange(
        to_later, to_earlier, centre, track_weight, point_weight
    )
    whole_track = whole_track.reshape(channels, track_weight.shape[1])
    block_out = (
        feat_wide
        + times_transposed(hidden[0], point_weight)
        + times_transposed(hidden[1], other_point)
    ).astype(jnp.bfloat16)
    scores = times(block_out, whole_track)
    cotangent = track_cotangent.reshape(number_rows, whole_track.shape[1])
    score_grad = (cotangent.astype(jnp.float32) * jax.nn.sigmoid(scores)).astype(jnp.bfloat16)
    own_part = times_transposed(score_grad, whole_track).astype(jnp.bfloat16)
    out_grad = own_part.astype(jnp.float32) + head_swap(own_part).astype(jnp.float32)
    out_grad_b = out_grad.astype(jnp.bfloat16)
    hidden_grad = times(out_grad_b, point_weight)
    middle_gradient = (hidden_grad * gelu_slope(middle)).astype(jnp.bfloat16)
    later, earlier = halo_exchange(middle_gradient)
    taps = (later, middle_gradient, earlier)
    blocks = [transposed_times(out_grad_b, hidden[0])] + [
        transposed_times(activated, tap) for tap in taps
    ]
    blocks = [block.astype(jnp.bfloat16) for block in blocks]
    grads = jnp.stack(
        [jnp.concatenate(blocks[:2], axis=1), jnp.concatenate(blocks[2:], axis=1)], axis=0
    )
    act_part = sum(times_transposed(tap, weight) for tap, weight in zip(taps, taps_weight))
    act_part = act_part.astype(jnp.bfloat16)
    summed, act_other = reduce_and_swap(grads, act_part)
    act_grad = act_part.astype(jnp.float32) + act_other.astype(jnp.float32)
    input_grad = (out_grad + act_grad * gelu_slope(feat_wide)).astype(jnp.bfloat16)
    point_grad = summed[0, :, :width]
    dilated_grad = jnp.stack(
        [summed[0, :, width:], summed[1, :, :width], summed[1, :, width:]], axis=1
    )
    return (input_grad.reshape(samples, positions, channels), dilated_grad, point_grad)


def solution(mesh):
    torus = Mesh(
        mesh.devices.reshape(NZ, NY, 2, mesh.shape["head"], mesh.shape["sample"]),
        ("z", "y", "c", "h", "s"),
    )
    placed = (
        P("s", SEQ, None),
        P(None, None, "h"),
        P(None, "h"),
        P("s", "h"),
        P("s", SEQ, "h"),
    )
    return jax.shard_map(
        body,
        mesh=torus,
        in_specs=placed,
        out_specs=(P("s", SEQ, None), P(SEQ_SAMPLE, None, "h"), P(SEQ_SAMPLE, "h")),
        check_vma=False,
    )
```

```python
import jax
import jax.numpy as jnp
from jax import lax
from jax.experimental import pallas as pl
from jax.experimental.pallas import tpu as pltpu
from jax.sharding import Mesh
from jax.sharding import PartitionSpec as P

MESH = pl.DeviceIdType.MESH
SEQ = ("z", "y", "c")
SEQ_SAMPLE = ("z", "y", "c", "s")
NZ, NY = 8, 4
YROWS, ZROWS = 64, 16
VMEM = pl.BlockSpec(memory_space=pltpu.VMEM)
ANY = pl.BlockSpec(memory_space=pl.ANY)
DMA = pltpu.SemaphoreType.DMA


def gelu_value(value):
    inner = 0.7978845608 * (value + 0.044715 * value * value * value)
    return 0.5 * value * (1.0 + jnp.tanh(inner))


def gelu_slope(value):
    inner = 0.7978845608 * (value + 0.044715 * value * value * value)
    tangent = jnp.tanh(inner)
    return 0.5 * (1.0 + tangent) + 0.5 * value * (1.0 - tangent * tangent) * 0.7978845608 * (
        1.0 + 3.0 * 0.044715 * value * value
    )


def times(left, right):
    return jnp.dot(left, right, preferred_element_type=jnp.float32)


def times_transposed(left, right):
    return lax.dot_general(
        left, right, (((1,), (1,)), ((), ())), preferred_element_type=jnp.float32
    )


def transposed_times(left, right):
    return lax.dot_general(
        left, right, (((0,), (0,)), ((), ())), preferred_element_type=jnp.float32
    )


def place():
    return tuple(lax.axis_index(name) for name in ("z", "y", "c", "h", "s"))


def remote(source, target, sent, arrived, **device):
    return pltpu.make_async_remote_copy(
        src_ref=source,
        dst_ref=target,
        send_sem=sent,
        recv_sem=arrived,
        device_id=device,
        device_id_type=MESH,
    )


def greet(barrier, **device):
    pl.semaphore_signal(barrier, inc=1, device_id=device, device_id_type=MESH)


def rows_at(start, size):
    return pl.ds(pl.multiple_of(start, 16), size)


def shifted(z, y, step):
    at = z * NY + y + step
    return {"z": lax.div(at, NY), "y": lax.rem(at, NY)}


def has_neighbours(z, y):
    at = z * NY + y
    return at >= 2, at < NZ * NY - 2


def send_halo(z, y, ahead, behind, sent, arrived):
    before, after = has_neighbours(z, y)

    @pl.when(after)
    def _():
        remote(*ahead, sent.at[0], arrived.at[0], **shifted(z, y, 2)).start()

    @pl.when(before)
    def _():
        remote(*behind, sent.at[1], arrived.at[1], **shifted(z, y, -2)).start()


def wait_halo(z, y, ahead, behind, sent, arrived):
    before, after = has_neighbours(z, y)

    @pl.when(before)
    def _():
        remote(*ahead, sent.at[0], arrived.at[0], c=lax.axis_index("c")).wait_recv()

    @pl.when(jnp.logical_not(before))
    def _():
        ahead[1][...] = jnp.zeros_like(ahead[1])

    @pl.when(after)
    def _():
        remote(*behind, sent.at[1], arrived.at[1], c=lax.axis_index("c")).wait_recv()

    @pl.when(jnp.logical_not(after))
    def _():
        behind[1][...] = jnp.zeros_like(behind[1])


def drain_halo(z, y, ahead, behind, sent, arrived):
    before, after = has_neighbours(z, y)

    @pl.when(after)
    def _():
        remote(*ahead, sent.at[0], arrived.at[0], c=lax.axis_index("c")).wait_send()

    @pl.when(before)
    def _():
        remote(*behind, sent.at[1], arrived.at[1], c=lax.axis_index("c")).wait_send()


def greet_halo(barrier, z, y):
    before, after = has_neighbours(z, y)

    @pl.when(after)
    def _():
        greet(barrier, **shifted(z, y, 2))

    @pl.when(before)
    def _():
        greet(barrier, **shifted(z, y, -2))

    return before.astype(jnp.int32) + after.astype(jnp.int32)


def forward_kernel(
    q0, q2, centre, tw, pw, middle, hidden, twf, pwo,
    from_before, from_after, own, own_sem,
    halo_s, halo_r, hid_s, hid_r, x_s, x_r, y_s, y_r, tz_s, tz_r, pz_s, pz_r, sib_s, sib_r,
):
    z, y, c, h, s = place()
    up, down = lax.rem(z + 1, NZ), lax.rem(z + NZ - 1, NZ)
    barrier = pltpu.get_barrier_semaphore()
    greet(barrier, h=1 - h)
    greet(barrier, s=1 - s)
    greet(barrier, c=1 - c)
    greet(barrier, z=up)
    greet(barrier, z=down)
    for step in range(1, NY):
        greet(barrier, y=lax.rem(y + step, NY))
    count = greet_halo(barrier, z, y)
    pl.semaphore_wait(barrier, 8 + count)

    half = tw.shape[0] // 2
    pw_rows = pw.shape[0] // 2 // NZ
    base = c * half

    def y_piece(at):
        return rows_at(base + at * YROWS, YROWS)

    def z_piece(at):
        return rows_at(base + NY * YROWS + at * ZROWS, ZROWS)

    def p_piece(at):
        return rows_at(c * (pw.shape[0] // 2) + at * pw_rows, pw_rows)

    ahead, behind = (q0, from_before), (q2, from_after)
    send_halo(z, y, ahead, behind, halo_s, halo_r)
    to_sample = [
        remote(tw.at[z_piece(z)], twf.at[s, z_piece(z)], x_s.at[0], x_r.at[0], s=1 - s),
        remote(tw.at[y_piece(y)], twf.at[s, y_piece(y)], x_s.at[1], x_r.at[1], s=1 - s),
    ]
    to_head = remote(pw.at[p_piece(z)], pwo.at[p_piece(z)], x_s.at[2], x_r.at[2], h=1 - h)
    to_sample[0].start()
    to_head.start()
    to_sample[1].start()
    take_own = pltpu.make_async_copy(tw, own, own_sem.at[0])
    take_own.start()

    started = [*to_sample, to_head]
    landed = []
    other = 1 - s

    def track_sibling(rows, slot):
        copy = remote(twf.at[other, rows], twf.at[other, rows], sib_s.at[slot], sib_r.at[slot], c=1 - c)
        copy.start()
        started.append(copy)

    def point_sibling(rows, slot):
        copy = remote(pwo.at[rows], pwo.at[rows], sib_s.at[slot], sib_r.at[slot], c=1 - c)
        copy.start()
        started.append(copy)

    def send_z(at, slot, target):
        rows = z_piece(at)
        copy = remote(twf.at[other, rows], twf.at[other, rows], tz_s.at[slot], tz_r.at[slot], z=target)
        copy.start()
        started.append(copy)

    def send_p(at, slot, target):
        rows = p_piece(at)
        copy = remote(pwo.at[rows], pwo.at[rows], pz_s.at[slot], pz_r.at[slot], z=target)
        copy.start()
        started.append(copy)

    to_sample[0].wait_recv()
    send_z(z, 0, up)
    send_z(z, 4, down)
    to_head.wait_recv()
    send_p(z, 0, up)
    send_p(z, 4, down)
    track_sibling(z_piece(z), 0)
    point_sibling(p_piece(z), 8)

    take_own.wait()
    put_own = pltpu.make_async_copy(own, twf.at[s], own_sem.at[1])
    put_own.start()

    def ring_step(step):
        for send, sem_s, sem_r, buf, piece, slot, sibling, first in (
            (send_z, tz_s, tz_r, None, z_piece, 0, track_sibling, 0),
            (send_p, pz_s, pz_r, pwo, p_piece, 0, point_sibling, 8),
        ):
            ref = twf.at[other] if buf is None else buf
            at = lax.rem(z + NZ - step, NZ)
            remote(ref.at[piece(at)], ref.at[piece(at)], sem_s.at[step - 1], sem_r.at[step - 1], z=up).wait_recv()
            if step < 4:
                send(at, step, up)
            sibling(piece(at), first + step)
            if step < 4:
                at = lax.rem(z + step, NZ)
                remote(ref.at[piece(at)], ref.at[piece(at)], sem_s.at[step + 3], sem_r.at[step + 3], z=up).wait_recv()
                if step < 3:
                    send(at, 4 + step, down)
                sibling(piece(at), first + 4 + step)

    ring_step(1)
    to_sample[1].wait_recv()
    rows = y_piece(y)
    for step in range(1, NY):
        copy = remote(
            twf.at[other, rows], twf.at[other, rows], y_s.at[step - 1], y_r.at[step - 1],
            y=lax.rem(y + step, NY),
        )
        copy.start()
        started.append(copy)
    track_sibling(rows, 16)
    ring_step(2)

    wait_halo(z, y, ahead, behind, halo_s, halo_r)
    total = centre[...] + from_before[...].astype(jnp.float32) + from_after[...].astype(jnp.float32)
    middle[...] = total
    hidden[0] = gelu_value(total).astype(jnp.bfloat16)
    to_partner = remote(hidden.at[0], hidden.at[1], hid_s, hid_r, h=1 - h)
    to_partner.start()
    started.append(to_partner)
    ring_step(3)
    ring_step(4)
    for step in range(1, NY):
        rows = y_piece(lax.rem(y + NY - step, NY))
        remote(
            twf.at[other, rows], twf.at[other, rows], y_s.at[step - 1], y_r.at[step - 1], y=y
        ).wait_recv()
        track_sibling(rows, 16 + step)
    to_partner.wait_recv()

    sib_base = (1 - c) * half
    sib_point = (1 - c) * (pw.shape[0] // 2)
    for slot in range(20):
        step = slot % 8 if slot < 16 else slot - 16
        if slot < 16:
            at = lax.rem(z + NZ - step, NZ) if step <= 4 else lax.rem(z + step - 4, NZ)
        else:
            at = lax.rem(y + NY - step, NY)
        if slot < 8:
            ref = twf.at[other, rows_at(sib_base + NY * YROWS + at * ZROWS, ZROWS)]
        elif slot < 16:
            ref = pwo.at[rows_at(sib_point + at * pw_rows, pw_rows)]
        else:
            ref = twf.at[other, rows_at(sib_base + at * YROWS, YROWS)]
        remote(ref, ref, sib_s.at[slot], sib_r.at[slot], c=1 - c).wait_recv()
    for copy in started:
        copy.wait_send()
    drain_halo(z, y, ahead, behind, halo_s, halo_r)
    put_own.wait()


def forward_exchange(q0, q2, centre, tw, pw):
    rows, width = q0.shape
    return pl.pallas_call(
        forward_kernel,
        out_shape=(
            jax.ShapeDtypeStruct((rows, width), jnp.float32),
            jax.ShapeDtypeStruct((2, rows, width), jnp.bfloat16),
            jax.ShapeDtypeStruct((2, *tw.shape), jnp.bfloat16),
            jax.ShapeDtypeStruct(pw.shape, jnp.bfloat16),
        ),
        in_specs=[VMEM, VMEM, VMEM, ANY, ANY],
        out_specs=(VMEM, VMEM, ANY, ANY),
        scratch_shapes=[
            pltpu.VMEM((rows, width), jnp.bfloat16),
            pltpu.VMEM((rows, width), jnp.bfloat16),
            pltpu.VMEM(tw.shape, jnp.bfloat16),
            DMA((2,)),
            DMA((2,)), DMA((2,)),
            DMA, DMA,
            DMA((3,)), DMA((3,)),
            DMA((3,)), DMA((3,)),
            DMA((7,)), DMA((7,)),
            DMA((7,)), DMA((7,)),
            DMA((20,)), DMA((20,)),
        ],
        compiler_params=pltpu.CompilerParams(collective_id=0, has_side_effects=True),
        name="forward_exchange",
    )(q0, q2, centre, tw, pw)


COLS = 256
HALVES, PIECES = 2, 2


def cols_at(start, size):
    return pl.ds(pl.multiple_of(start, 128), size)


def repeat(count, step, start=0):
    def once(at, carry):
        step(at)
        return carry

    lax.fori_loop(start, count, once, 0)


def backward_kernel(
    feat, hidden, middle, act_t, tw, cot, pw, pwo, w3, grad_out, summed,
    v_feat, v_act, v_tw, v_cot, v_pw, v_pwo, v_w3, block, score, out_grad, slope_f, slope_m,
    hid_grad, mid_grad, later, earlier, swap_out, swap_in, act_out, act_in,
    early, late, sib_early, sib_late, ring_out, ring_in, final, early_out, early_in,
    y_out, y_in, z_tile, z_out, z_in,
    load, tw_load, swap_s, swap_r, acts_s, acts_r, halo_s, halo_r, sibe_s, sibe_r, sibl_s, sibl_r,
    ring_s, ring_r, fin_s, fin_r, y_s, y_r, z_s, z_r,
):
    z, y, c, h, s = place()
    up, down = lax.rem(z + 1, NZ), lax.rem(z + NZ - 1, NZ)
    me = (y * 2 + c) * 2 + s
    corner = c * 2 + s
    channels, tracks = tw.shape
    chunks = channels // COLS
    rows = channels // NZ
    part = rows // NY
    each = part // 4
    sub = rows // HALVES // PIECES
    bf16, f32 = jnp.bfloat16, jnp.float32

    def group(at):
        return {"y": lax.div(at, 4), "c": lax.rem(lax.div(at, 2), 2), "s": lax.rem(at, 2)}

    def corner_of(at):
        return {"c": lax.div(at, 2), "s": lax.rem(at, 2)}

    barrier = pltpu.get_barrier_semaphore()
    greet(barrier, h=1 - h)
    for step in range(1, 16):
        greet(barrier, **group(lax.rem(me + step, 16)))
    for step in range(1, NZ):
        for turn in range(4):
            greet(barrier, z=lax.rem(z + step, NZ), **corner_of(turn))
    greeted = 1 + 15 + 4 * (NZ - 1) + greet_halo(barrier, z, y)

    loads = [
        pltpu.make_async_copy(source, target, load.at[slot])
        for slot, (source, target) in enumerate(
            ((feat, v_feat), (pw, v_pw), (pwo, v_pwo), (cot, v_cot), (act_t, v_act), (w3, v_w3))
        )
    ]
    whole, tail = tracks // COLS, tracks % COLS

    def tw_copy(at, size=COLS):
        where = cols_at(at * COLS, size)
        return pltpu.make_async_copy(tw.at[:, where], v_tw.at[:, where], tw_load.at[at])

    for copy in loads[:3]:
        copy.start()
    repeat(whole, lambda at: tw_copy(at).start())
    tw_copy(whole, tail).start()
    for copy in loads[3:]:
        copy.start()
    for copy in loads[:3]:
        copy.wait()

    def block_step(at):
        cols, where = cols_at(at * COLS, COLS), rows_at(at * COLS, COLS)
        value = v_feat[:, cols].astype(f32)
        value = value + times_transposed(hidden[0], v_pw[where, :])
        value = value + times_transposed(hidden[1], v_pwo[where, :])
        block[:, cols] = value.astype(bf16)

    repeat(chunks, block_step)
    loads[3].wait()

    def score_step(at, size=COLS):
        tw_copy(at, size).wait()
        cols = cols_at(at * COLS, size)
        value = jax.nn.sigmoid(times(block[...], v_tw[:, cols]))
        score[:, cols] = (v_cot[:, cols].astype(f32) * value).astype(bf16)

    repeat(whole, score_step)
    score_step(whole, tail)
    pl.semaphore_wait(barrier, greeted)

    def swap_copy(at):
        return remote(swap_out.at[at], swap_in.at[at], swap_s.at[at], swap_r.at[at], h=1 - h)

    def swap_step(at):
        swap_out[at] = times_transposed(score[...], v_tw[rows_at(at * COLS, COLS), :]).astype(bf16)
        swap_copy(at).start()

    repeat(chunks, swap_step)
    slope_m[...] = gelu_slope(middle[...])
    hid_grad[...] = jnp.zeros_like(hid_grad)

    def slope_step(at):
        cols = cols_at(at * COLS, COLS)
        slope_f[at] = gelu_slope(v_feat[:, cols].astype(f32))

    repeat(chunks, slope_step)

    def gather_step(at):
        swap_copy(at).wait_recv()
        where = rows_at(at * COLS, COLS)
        value = swap_out[at].astype(f32) + swap_in[at].astype(f32)
        out_grad[at] = value
        rounded = value.astype(bf16)
        hid_grad[...] += times(rounded, v_pw[where, :])
        early[0, where, :] = transposed_times(rounded, hidden[0]).astype(bf16)

    repeat(chunks, gather_step)
    mid_grad[...] = (hid_grad[...] * slope_m[...]).astype(bf16)
    ahead, behind = (mid_grad, earlier), (mid_grad, later)
    send_halo(z, y, ahead, behind, halo_s, halo_r)

    loads[4].wait()

    def centre_step(at):
        where = rows_at(at * rows, rows)
        early[1, where, :] = times(v_act[where, :], mid_grad[...]).astype(bf16)

    repeat(NZ, centre_step)
    order = (7, 1, 6, 2, 5, 3, 4, 0)

    def early_sibling(slot):
        where = rows_at(lax.rem(z + order[slot], NZ) * rows, rows)
        return remote(early.at[1 - c, where], sib_early.at[where], sibe_s.at[slot], sibe_r.at[slot], c=1 - c)

    for slot in range(NZ):
        early_sibling(slot).start()

    def partial(at, way, piece):
        where = rows_at(at * rows + (way * PIECES + piece) * sub, sub)
        return early[c, where, :].astype(f32) + sib_early[where, :].astype(f32)

    def ring_copy(step, way, piece):
        return remote(
            ring_out.at[step, way, piece], ring_in.at[step, way, piece],
            ring_s.at[step, way, piece], ring_r.at[step, way, piece], z=up if way == 0 else down,
        )

    def ring_step(step):
        for piece in range(PIECES):
            for way in range(HALVES):
                at = lax.rem(z + NZ - 1 - step, NZ) if way == 0 else lax.rem(z + 1 + step, NZ)
                value = partial(at, way, piece)
                if step:
                    ring_copy(step - 1, way, piece).wait_recv()
                    value = value + ring_in[step - 1, way, piece].astype(f32)
                ring_out[step, way, piece] = value.astype(bf16)
                ring_copy(step, way, piece).start()

    early_sibling(0).wait_recv()
    early_sibling(1).wait_recv()
    ring_step(0)
    for slot in range(2, NZ):
        early_sibling(slot).wait_recv()
    ring_step(1)
    ring_step(2)
    wait_halo(z, y, ahead, behind, halo_s, halo_r)

    def late_sibling(at):
        where = rows_at(at * rows, rows)
        return remote(late.at[1 - c, where], sib_late.at[where], sibl_s.at[at], sibl_r.at[at], c=1 - c)

    def late_step(turn):
        at = lax.rem(z + turn, NZ)
        where = rows_at(at * rows, rows)
        late[0, where, :] = times(v_act[where, :], later[...]).astype(bf16)
        late[1, where, :] = times(v_act[where, :], earlier[...]).astype(bf16)
        late_sibling(at).start()

    def y_copy(at, step):
        return remote(
            y_out.at[at, rows_at(lax.rem(y + step, NY) * part, part)], y_in.at[at, step - 1],
            y_s.at[at, step - 1], y_r.at[at, step - 1], y=lax.rem(y + step, NY),
        )

    def y_step(turn):
        at = lax.rem(z + turn, NZ)
        where = rows_at(at * rows, rows)
        late_sibling(at).wait_recv()
        y_out[at] = (late[c, where, :].astype(f32) + sib_late[where, :].astype(f32)).astype(bf16)
        for step in range(1, NY):
            y_copy(at, step).start()

    def late_and_y_step(turn):
        late_step(turn)
        y_step(turn - 1)

    late_step(1)
    repeat(NZ + 1, late_and_y_step, 2)
    y_step(NZ)
    ring_step(3)
    loads[5].wait()

    def act_copy(at):
        return remote(act_out.at[at], act_in.at[at], acts_s.at[at], acts_r.at[at], h=1 - h)

    def act_step(at):
        where = rows_at(at * COLS, COLS)
        value = times_transposed(later[...], v_w3[0, where, :])
        value = value + times_transposed(mid_grad[...], v_w3[1, where, :])
        value = value + times_transposed(earlier[...], v_w3[2, where, :])
        act_out[at] = value.astype(bf16)
        act_copy(at).start()

    repeat(chunks, act_step)
    ring_step(4)

    def z_copy(turn, at, twist):
        to = lax.rem(corner + twist, 4)
        return remote(
            z_out.at[at, to], z_in.at[z, corner], z_s.at[turn - 1, twist], z_r.at[turn - 1, twist],
            z=at, **corner_of(to),
        )

    def z_sum(turn):
        at = lax.rem(z + turn, NZ)
        where = rows_at(at * rows + y * part, part)
        value = late[c, where, :].astype(f32) + sib_late[where, :].astype(f32)
        for step in range(1, NY):
            y_copy(at, step).wait_recv()
            value = value + y_in[at, step - 1].astype(f32)
        z_tile[...] = value
        for to in range(4):
            z_out[at, to] = z_tile[to * each:(to + 1) * each, :].astype(bf16)
        return at

    def z_step(turn):
        at = z_sum(turn)
        for twist in range(4):
            z_copy(turn, at, twist).start()

    z_step(1)
    z_step(2)
    ring_step(5)
    z_step(3)
    z_step(4)
    ring_step(6)
    z_step(5)
    z_step(6)
    z_step(7)
    z_sum(NZ)
    for twist in range(1, 4):
        z_copy(NZ, z, twist).start()
    z_in[z, corner] = z_out[z, corner]

    for piece in range(PIECES):
        for way in range(HALVES):
            value = partial(z, way, piece)
            ring_copy(NZ - 2, way, piece).wait_recv()
            value = value + ring_in[NZ - 2, way, piece].astype(f32)
            final[(way * PIECES + piece) * sub:(way * PIECES + piece + 1) * sub, :] = value
    for at in range(16):
        early_out[at] = final[at * each:(at + 1) * each, :].astype(bf16)

    def fin_copy(step):
        to = lax.rem(me + step, 16)
        return remote(early_out.at[to], early_in.at[me], fin_s.at[step - 1], fin_r.at[step - 1], **group(to))

    for step in range(1, 16):
        fin_copy(step).start()
    early_in[me] = early_out[me]

    def out_step(at):
        act_copy(at).wait_recv()
        value = act_out[at].astype(f32) + act_in[at].astype(f32)
        grad_out[:, cols_at(at * COLS, COLS)] = (out_grad[at] + value * slope_f[at]).astype(bf16)

    repeat(chunks, out_step)
    for turn in range(1, NZ + 1):
        for twist in range(1 if turn == NZ else 0, 4):
            source = lax.rem(z + 2 * NZ - turn, NZ)
            ref = z_in.at[source, lax.rem(corner + 4 - twist, 4)]
            remote(ref, ref, z_s.at[turn - 1, twist], z_r.at[turn - 1, twist], z=z).wait_recv()
    for core in range(2):
        total = jnp.zeros((each, hidden.shape[2]), f32)
        for turn in range(NZ):
            for sample in range(2):
                total = total + z_in[turn, core * 2 + sample].astype(f32)
        summed[2 + core] = total
    for step in range(1, 16):
        ref = early_in.at[lax.rem(me + 16 - step, 16)]
        remote(ref, ref, fin_s.at[step - 1], fin_r.at[step - 1], z=z).wait_recv()
    for core in range(2):
        total = jnp.zeros((each, hidden.shape[2]), f32)
        for row in range(NY):
            for sample in range(2):
                total = total + early_in[(row * 2 + core) * 2 + sample].astype(f32)
        summed[core] = total

    def drain_chunks(at):
        swap_copy(at).wait_send()
        act_copy(at).wait_send()

    repeat(chunks, drain_chunks)
    drain_halo(z, y, ahead, behind, halo_s, halo_r)
    for slot in range(NZ):
        early_sibling(slot).wait_send()
    for step in range(NZ - 1):
        for piece in range(PIECES):
            for way in range(HALVES):
                ring_copy(step, way, piece).wait_send()

    def drain_late(at):
        late_sibling(at).wait_send()
        for step in range(1, NY):
            y_copy(at, step).wait_send()

    repeat(NZ, drain_late)
    for turn in range(1, NZ + 1):
        for twist in range(1 if turn == NZ else 0, 4):
            z_copy(turn, lax.rem(z + turn, NZ), twist).wait_send()
    for step in range(1, 16):
        fin_copy(step).wait_send()


def backward(feat, hidden, middle, act_t, tw, cot, pw, pwo, w3):
    bf16, f32 = jnp.bfloat16, jnp.float32
    positions, channels = feat.shape
    width = pw.shape[1]
    tracks = tw.shape[1]
    chunks = channels // COLS
    rows = channels // NZ
    part = rows // NY
    each = part // 4
    sub = rows // HALVES // PIECES
    ring = (NZ - 1, HALVES, PIECES)
    tile = (chunks, positions, COLS)
    return pl.pallas_call(
        backward_kernel,
        out_shape=(
            jax.ShapeDtypeStruct((positions, channels), bf16),
            jax.ShapeDtypeStruct((4, each, width), f32),
        ),
        in_specs=[ANY, VMEM, VMEM, ANY, ANY, ANY, ANY, ANY, ANY],
        out_specs=(VMEM, VMEM),
        scratch_shapes=[
            pltpu.VMEM(feat.shape, bf16),
            pltpu.VMEM(act_t.shape, bf16),
            pltpu.VMEM(tw.shape, bf16),
            pltpu.VMEM(cot.shape, bf16),
            pltpu.VMEM(pw.shape, bf16),
            pltpu.VMEM(pwo.shape, bf16),
            pltpu.VMEM(w3.shape, bf16),
            pltpu.VMEM((positions, channels), bf16),
            pltpu.VMEM((positions, tracks), bf16),
            pltpu.VMEM(tile, f32),
            pltpu.VMEM(tile, f32),
            pltpu.VMEM((positions, width), f32),
            pltpu.VMEM((positions, width), f32),
            pltpu.VMEM((positions, width), bf16),
            pltpu.VMEM((positions, width), bf16),
            pltpu.VMEM((positions, width), bf16),
            pltpu.VMEM(tile, bf16),
            pltpu.VMEM(tile, bf16),
            pltpu.VMEM(tile, bf16),
            pltpu.VMEM(tile, bf16),
            pltpu.VMEM((2, channels, width), bf16),
            pltpu.VMEM((2, channels, width), bf16),
            pltpu.VMEM((channels, width), bf16),
            pltpu.VMEM((channels, width), bf16),
            pltpu.VMEM((*ring, sub, width), bf16),
            pltpu.VMEM((*ring, sub, width), bf16),
            pltpu.VMEM((rows, width), f32),
            pltpu.VMEM((16, each, width), bf16),
            pltpu.VMEM((16, each, width), bf16),
            pltpu.VMEM((NZ, rows, width), bf16),
            pltpu.VMEM((NZ, NY - 1, part, width), bf16),
            pltpu.VMEM((part, width), f32),
            pltpu.VMEM((NZ, 4, each, width), bf16),
            pltpu.VMEM((NZ, 4, each, width), bf16),
            DMA((6,)), DMA((tracks // COLS + 1,)),
            DMA((chunks,)), DMA((chunks,)),
            DMA((chunks,)), DMA((chunks,)),
            DMA((2,)), DMA((2,)),
            DMA((NZ,)), DMA((NZ,)),
            DMA((NZ,)), DMA((NZ,)),
            DMA(ring), DMA(ring),
            DMA((15,)), DMA((15,)),
            DMA((NZ, NY - 1)), DMA((NZ, NY - 1)),
            DMA((NZ, 4)), DMA((NZ, 4)),
        ],
        compiler_params=pltpu.CompilerParams(
            collective_id=1, has_side_effects=True, vmem_limit_bytes=60 * 1024 * 1024
        ),
        name="backward",
    )(feat, hidden, middle, act_t, tw, cot, pw, pwo, w3)


def body(features, dilated_weight, point_weight, track_weight, track_cotangent):
    samples, positions, channels = features.shape
    number_rows = samples * positions
    width = dilated_weight.shape[2]
    feat = features.reshape(number_rows, channels)
    activated = gelu_value(feat.astype(jnp.float32)).astype(jnp.bfloat16)
    taps_weight = jnp.transpose(dilated_weight, (1, 0, 2))
    to_later = times(activated, taps_weight[0]).astype(jnp.bfloat16)
    to_earlier = times(activated, taps_weight[2]).astype(jnp.bfloat16)
    centre = times(activated, taps_weight[1])
    middle, hidden, whole_track, other_point = forward_exchange(
        to_later, to_earlier, centre, track_weight, point_weight
    )
    whole_track = whole_track.reshape(channels, track_weight.shape[1])
    cotangent = track_cotangent.reshape(number_rows, whole_track.shape[1])
    input_grad, summed = backward(
        feat, hidden, middle, activated.T, whole_track, cotangent, point_weight, other_point,
        taps_weight,
    )
    dilated_grad = jnp.stack([summed[2], summed[1], summed[3]], axis=1)
    return (input_grad.reshape(samples, positions, channels), dilated_grad, summed[0])


def solution(mesh):
    torus = Mesh(
        mesh.devices.reshape(NZ, NY, 2, mesh.shape["head"], mesh.shape["sample"]),
        ("z", "y", "c", "h", "s"),
    )
    placed = (
        P("s", SEQ, None),
        P(None, None, "h"),
        P(None, "h"),
        P("s", "h"),
        P("s", SEQ, "h"),
    )
    return jax.shard_map(
        body,
        mesh=torus,
        in_specs=placed,
        out_specs=(P("s", SEQ, None), P(SEQ_SAMPLE, None, "h"), P(SEQ_SAMPLE, "h")),
        check_vma=False,
    )
```

```python
import jax
import jax.numpy as jnp
from jax import lax
from jax.experimental import pallas as pl
from jax.experimental.pallas import tpu as pltpu
from jax.sharding import Mesh
from jax.sharding import PartitionSpec as P

MESH = pl.DeviceIdType.MESH
SEQ = ("z", "y", "c")
SEQ_SAMPLE = ("z", "y", "c", "s")
NZ, NY = 8, 4
VMEM = pl.BlockSpec(memory_space=pltpu.VMEM)
ANY = pl.BlockSpec(memory_space=pltpu.HBM)
DMA = pltpu.SemaphoreType.DMA


def gelu_value(value):
    inner = 0.7978845608 * (value + 0.044715 * value * value * value)
    return 0.5 * value * (1.0 + jnp.tanh(inner))


def gelu_slope(value):
    inner = 0.7978845608 * (value + 0.044715 * value * value * value)
    tangent = jnp.tanh(inner)
    return 0.5 * (1.0 + tangent) + 0.5 * value * (1.0 - tangent * tangent) * 0.7978845608 * (
        1.0 + 3.0 * 0.044715 * value * value
    )


def times(left, right):
    return jnp.dot(left, right, preferred_element_type=jnp.float32)


def times_transposed(left, right):
    return lax.dot_general(
        left, right, (((1,), (1,)), ((), ())), preferred_element_type=jnp.float32
    )


def transposed_times(left, right):
    return lax.dot_general(
        left, right, (((0,), (0,)), ((), ())), preferred_element_type=jnp.float32
    )


def place():
    return tuple(lax.axis_index(name) for name in ("z", "y", "c", "h", "s"))


def remote(source, target, sent, arrived, **device):
    return pltpu.make_async_remote_copy(
        src_ref=source,
        dst_ref=target,
        send_sem=sent,
        recv_sem=arrived,
        device_id=device,
        device_id_type=MESH,
    )


def greet(barrier, **device):
    pl.semaphore_signal(barrier, inc=1, device_id=device, device_id_type=MESH)


def rows_at(start, size):
    return pl.ds(pl.multiple_of(start, 16), size)


def shifted(z, y, step):
    at = z * NY + y + step
    return {"z": lax.div(at, NY), "y": lax.rem(at, NY)}


def has_neighbours(z, y):
    at = z * NY + y
    return at >= 2, at < NZ * NY - 2


def send_halo(z, y, ahead, behind, sent, arrived):
    before, after = has_neighbours(z, y)

    @pl.when(after)
    def _():
        remote(*ahead, sent.at[0], arrived.at[0], **shifted(z, y, 2)).start()

    @pl.when(before)
    def _():
        remote(*behind, sent.at[1], arrived.at[1], **shifted(z, y, -2)).start()


def wait_halo(z, y, ahead, behind, sent, arrived):
    before, after = has_neighbours(z, y)

    @pl.when(before)
    def _():
        remote(*ahead, sent.at[0], arrived.at[0], c=lax.axis_index("c")).wait_recv()

    @pl.when(jnp.logical_not(before))
    def _():
        ahead[1][...] = jnp.zeros_like(ahead[1])

    @pl.when(after)
    def _():
        remote(*behind, sent.at[1], arrived.at[1], c=lax.axis_index("c")).wait_recv()

    @pl.when(jnp.logical_not(after))
    def _():
        behind[1][...] = jnp.zeros_like(behind[1])


def drain_halo(z, y, ahead, behind, sent, arrived):
    before, after = has_neighbours(z, y)

    @pl.when(after)
    def _():
        remote(*ahead, sent.at[0], arrived.at[0], c=lax.axis_index("c")).wait_send()

    @pl.when(before)
    def _():
        remote(*behind, sent.at[1], arrived.at[1], c=lax.axis_index("c")).wait_send()


def greet_halo(barrier, z, y):
    before, after = has_neighbours(z, y)

    @pl.when(after)
    def _():
        greet(barrier, **shifted(z, y, 2))

    @pl.when(before)
    def _():
        greet(barrier, **shifted(z, y, -2))

    return before.astype(jnp.int32) + after.astype(jnp.int32)


COLS = 256
HALVES, PIECES = 2, 2


def cols_at(start, size):
    return pl.ds(pl.multiple_of(start, 128), size)


def repeat(count, step, start=0):
    def once(at, carry):
        step(at)
        return carry

    lax.fori_loop(start, count, once, 0)


YROWS, ZROWS, ZCUT = 40, 56, 32


def forward_kernel(
    feat, w3, tw, pw, middle, hid_own, block, act_t, twf,
    v_feat, v_w3, v_pw, own, act, ahead_out, behind_out, from_before, from_after, centre, hid_other, pwo,
    load, own_sem, halo_s, halo_r, hid_s, hid_r, x_s, x_r, y_s, y_r, pz_s, pz_r, tz_s, tz_r, sib_s, sib_r,
):
    z, y, c, h, s = place()
    bf16, f32 = jnp.bfloat16, jnp.float32
    channels = feat.shape[1]
    chunks = channels // COLS
    barrier = pltpu.get_barrier_semaphore()
    greet(barrier, h=1 - h)
    greet(barrier, s=1 - s)
    greet(barrier, c=1 - c)
    for step in (1, 2, NZ - 2, NZ - 1):
        greet(barrier, z=lax.rem(z + step, NZ))
    for step in range(1, NY):
        greet(barrier, y=lax.rem(y + step, NY))
    greeted = 10 + greet_halo(barrier, z, y)
    loads = [
        pltpu.make_async_copy(source, target, load.at[slot])
        for slot, (source, target) in enumerate(
            ((feat, v_feat), (w3.at[0], v_w3.at[0]), (w3.at[2], v_w3.at[2]), (w3.at[1], v_w3.at[1]), (pw, v_pw))
        )
    ]
    for copy in loads:
        copy.start()
    take_own = pltpu.make_async_copy(tw, own, own_sem.at[0])
    take_own.start()

    half = tw.shape[0] // 2
    point = pw.shape[0] // 2
    p_rows = point // 4
    other = 1 - s

    def rows8(start, size):
        return pl.ds(pl.multiple_of(start, 8), size)

    def y_rows(core, at):
        return rows8(core * half + at * YROWS, YROWS)

    def z_rows(core, at, cut):
        start = core * half + NY * YROWS + lax.rem(at, 4) * ZROWS
        return rows8(start, ZCUT) if cut == 0 else rows8(start + ZCUT, ZROWS - ZCUT)

    def p_rows_of(core, at, cut):
        start = core * point + lax.rem(at, 4) * p_rows
        if cut is None:
            return rows8(start, p_rows)
        return rows8(start + cut * (p_rows // 2), p_rows // 2)

    started = []

    def go(ref, target, sent, arrived, **device):
        copy = remote(ref, target, sent, arrived, **device)
        copy.start()
        started.append(copy)

    def landing(ref, sent, arrived):
        remote(ref, ref, sent, arrived, c=1 - c).wait_recv()

    pl.semaphore_wait(barrier, greeted)
    here = p_rows_of(c, z, None)
    go(pw.at[here], pwo.at[here], x_s.at[0], x_r.at[0], h=1 - h)
    for cut in range(2):
        here = z_rows(c, z, cut)
        go(tw.at[here], twf.at[s, here], x_s.at[1 + cut], x_r.at[1 + cut], s=1 - s)
    here = y_rows(c, y)
    go(tw.at[here], twf.at[s, here], x_s.at[3], x_r.at[3], s=1 - s)

    loads[0].wait()

    def act_step(at):
        cols = cols_at(at * COLS, COLS)
        act[:, cols] = gelu_value(v_feat[:, cols].astype(f32)).astype(bf16)

    repeat(chunks, act_step)
    before, after = has_neighbours(z, y)
    ahead, behind = (ahead_out, from_before), (behind_out, from_after)
    loads[1].wait()
    ahead_out[...] = times(act[...], v_w3[0]).astype(bf16)

    @pl.when(after)
    def _():
        remote(*ahead, halo_s.at[0], halo_r.at[0], **shifted(z, y, 2)).start()

    loads[2].wait()
    behind_out[...] = times(act[...], v_w3[2]).astype(bf16)

    @pl.when(before)
    def _():
        remote(*behind, halo_s.at[1], halo_r.at[1], **shifted(z, y, -2)).start()

    steps = (1, NZ - 1, 2, NZ - 2)
    here = pwo.at[p_rows_of(c, z, None)]
    landing(here, x_s.at[0], x_r.at[0])
    for slot in range(2):
        go(here, here, pz_s.at[slot], pz_r.at[slot], z=lax.rem(z + steps[slot], NZ))
    for cut in range(2):
        piece = pwo.at[p_rows_of(c, z, cut)]
        go(piece, piece, pz_s.at[2 + cut], pz_r.at[2 + cut], z=lax.rem(z + steps[2 + cut], NZ))
    go(here, here, sib_s.at[0], sib_r.at[0], c=1 - c)
    for cut in range(2):
        here = twf.at[other, z_rows(c, z, cut)]
        landing(here, x_s.at[1 + cut], x_r.at[1 + cut])
        for slot, step in enumerate((steps[0], steps[1], steps[2 + cut])):
            go(here, here, tz_s.at[cut, slot], tz_r.at[cut, slot], z=lax.rem(z + step, NZ))
        go(here, here, sib_s.at[5 + cut], sib_r.at[5 + cut], c=1 - c)
        if cut == 0:
            loads[3].wait()
            centre[...] = times(act[...], v_w3[1])
    here = twf.at[other, y_rows(c, y)]
    landing(here, x_s.at[3], x_r.at[3])
    for step in range(1, NY):
        go(here, here, y_s.at[step - 1], y_r.at[step - 1], y=lax.rem(y + step, NY))
    go(here, here, sib_s.at[13], sib_r.at[13], c=1 - c)
    take_own.wait()
    put_own = pltpu.make_async_copy(own, twf.at[s], own_sem.at[1])
    put_own.start()

    def turn_step(at):
        act_t[rows_at(at * COLS, COLS), :] = act[:, cols_at(at * COLS, COLS)].T

    repeat(chunks, turn_step)

    def p_from(core, slot):
        at = z + NZ - steps[slot]
        return pwo.at[p_rows_of(core, at, None if slot < 2 else slot - 2)]

    def t_from(core, cut, slot):
        step = steps[slot] if slot < 2 else steps[2 + cut]
        return twf.at[other, z_rows(core, z + NZ - step, cut)]

    def y_from(core, step):
        return twf.at[other, y_rows(core, lax.rem(y + NY - step, NY))]

    for slot in range(4):
        here = p_from(c, slot)
        landing(here, pz_s.at[slot], pz_r.at[slot])
        go(here, here, sib_s.at[1 + slot], sib_r.at[1 + slot], c=1 - c)

    wait_halo(z, y, ahead, behind, halo_s, halo_r)
    total = centre[...] + from_before[...].astype(f32) + from_after[...].astype(f32)
    middle[...] = total
    hid_own[...] = gelu_value(total).astype(bf16)
    go(hid_own, hid_other, hid_s, hid_r, h=1 - h)

    for cut in range(2):
        for slot in range(3):
            here = t_from(c, cut, slot)
            landing(here, tz_s.at[cut, slot], tz_r.at[cut, slot])
            at = 7 + cut * 3 + slot
            go(here, here, sib_s.at[at], sib_r.at[at], c=1 - c)
    for step in range(1, NY):
        here = y_from(c, step)
        landing(here, y_s.at[step - 1], y_r.at[step - 1])
        go(here, here, sib_s.at[13 + step], sib_r.at[13 + step], c=1 - c)

    landing(pwo.at[p_rows_of(1 - c, z, None)], sib_s.at[0], sib_r.at[0])
    for slot in range(4):
        landing(p_from(1 - c, slot), sib_s.at[1 + slot], sib_r.at[1 + slot])
    loads[4].wait()
    landing(hid_other, hid_s, hid_r)

    def block_step(at):
        cols, where = cols_at(at * COLS, COLS), rows_at(at * COLS, COLS)
        value = v_feat[:, cols].astype(f32)
        value = value + times_transposed(hid_own[...], v_pw[where, :])
        value = value + times_transposed(hid_other[...], pwo[where, :])
        block[:, cols] = value.astype(bf16)

    repeat(chunks, block_step)
    for cut in range(2):
        landing(twf.at[other, z_rows(1 - c, z, cut)], sib_s.at[5 + cut], sib_r.at[5 + cut])
        for slot in range(3):
            at = 7 + cut * 3 + slot
            landing(t_from(1 - c, cut, slot), sib_s.at[at], sib_r.at[at])
    landing(twf.at[other, y_rows(1 - c, y)], sib_s.at[13], sib_r.at[13])
    for step in range(1, NY):
        landing(y_from(1 - c, step), sib_s.at[13 + step], sib_r.at[13 + step])
    for copy in started:
        copy.wait_send()
    drain_halo(z, y, ahead, behind, halo_s, halo_r)
    put_own.wait()


def forward_exchange(feat, w3, tw, pw):
    bf16, f32 = jnp.bfloat16, jnp.float32
    positions, channels = feat.shape
    width = pw.shape[1]
    return pl.pallas_call(
        forward_kernel,
        out_shape=(
            jax.ShapeDtypeStruct((positions, width), f32),
            jax.ShapeDtypeStruct((positions, width), bf16),
            jax.ShapeDtypeStruct((positions, channels), bf16),
            jax.ShapeDtypeStruct((channels, positions), bf16),
            jax.ShapeDtypeStruct((2, *tw.shape), bf16),
        ),
        in_specs=[ANY, ANY, ANY, ANY],
        out_specs=(VMEM, VMEM, VMEM, VMEM, ANY),
        scratch_shapes=[
            pltpu.VMEM(feat.shape, bf16),
            pltpu.VMEM(w3.shape, bf16),
            pltpu.VMEM(pw.shape, bf16),
            pltpu.VMEM(tw.shape, bf16),
            pltpu.VMEM(feat.shape, bf16),
            pltpu.VMEM((positions, width), bf16),
            pltpu.VMEM((positions, width), bf16),
            pltpu.VMEM((positions, width), bf16),
            pltpu.VMEM((positions, width), bf16),
            pltpu.VMEM((positions, width), f32),
            pltpu.VMEM((positions, width), bf16),
            pltpu.VMEM(pw.shape, bf16),
            DMA((5,)), DMA((2,)),
            DMA((2,)), DMA((2,)),
            DMA, DMA,
            DMA((4,)), DMA((4,)),
            DMA((3,)), DMA((3,)),
            DMA((4,)), DMA((4,)),
            DMA((2, 3)), DMA((2, 3)),
            DMA((17,)), DMA((17,)),
        ],
        compiler_params=pltpu.CompilerParams(
            collective_id=0, has_side_effects=True, vmem_limit_bytes=67043328
        ),
        name="forward_exchange",
    )(feat, w3, tw, pw)


def backward_kernel(
    feat, hidden, middle, block_hbm, act_hbm, tw, cot, pw, w3, grad_out, summed,
    v_feat, block, act_t, v_tw, v_cot, v_pw, v_w3, score, out_grad, slope_f, slope_m,
    hid_grad, mid_grad, later, earlier, swap_out, swap_in, act_out, act_in,
    early, late, sib_early, sib_late, ring_out, ring_in, final, early_out, early_in,
    y_out, y_in, z_tile, z_out, z_in,
    load, tw_load, swap_s, swap_r, acts_s, acts_r, halo_s, halo_r, sibe_s, sibe_r, sibl_s, sibl_r,
    ring_s, ring_r, fin_s, fin_r, y_s, y_r, z_s, z_r,
):
    z, y, c, h, s = place()
    up, down = lax.rem(z + 1, NZ), lax.rem(z + NZ - 1, NZ)
    me = (y * 2 + c) * 2 + s
    corner = c * 2 + s
    channels, tracks = tw.shape
    chunks = channels // COLS
    rows = channels // NZ
    part = rows // NY
    each = part // 4
    sub = rows // HALVES // PIECES
    bf16, f32 = jnp.bfloat16, jnp.float32

    def group(at):
        return {"y": lax.div(at, 4), "c": lax.rem(lax.div(at, 2), 2), "s": lax.rem(at, 2)}

    def corner_of(at):
        return {"c": lax.div(at, 2), "s": lax.rem(at, 2)}

    barrier = pltpu.get_barrier_semaphore()
    greet(barrier, h=1 - h)
    for step in range(1, 16):
        greet(barrier, **group(lax.rem(me + step, 16)))
    for step in range(1, NZ):
        for turn in range(4):
            greet(barrier, z=lax.rem(z + step, NZ), **corner_of(turn))
    greeted = 1 + 15 + 4 * (NZ - 1) + greet_halo(barrier, z, y)

    loads = [
        pltpu.make_async_copy(source, target, load.at[slot])
        for slot, (source, target) in enumerate(
            ((block_hbm, block), (cot, v_cot), (feat, v_feat), (pw, v_pw), (act_hbm, act_t), (w3, v_w3))
        )
    ]
    whole, tail = tracks // COLS, tracks % COLS

    def tw_copy(at, size=COLS):
        where = cols_at(at * COLS, size)
        return pltpu.make_async_copy(tw.at[:, where], v_tw.at[:, where], tw_load.at[at])

    loads[0].start()
    repeat(whole, lambda at: tw_copy(at).start())
    tw_copy(whole, tail).start()
    for copy in loads[1:]:
        copy.start()
    loads[0].wait()
    loads[1].wait()

    def score_step(at, size=COLS):
        tw_copy(at, size).wait()
        cols = cols_at(at * COLS, size)
        value = jax.nn.sigmoid(times(block[...], v_tw[:, cols]))
        score[:, cols] = (v_cot[:, cols].astype(f32) * value).astype(bf16)

    repeat(whole, score_step)
    score_step(whole, tail)
    pl.semaphore_wait(barrier, greeted)

    def swap_copy(at):
        return remote(swap_out.at[at], swap_in.at[at], swap_s.at[at], swap_r.at[at], h=1 - h)

    def swap_step(at):
        swap_out[at] = times_transposed(score[...], v_tw[rows_at(at * COLS, COLS), :]).astype(bf16)
        swap_copy(at).start()

    repeat(chunks, swap_step)
    loads[2].wait()
    loads[3].wait()
    slope_m[...] = gelu_slope(middle[...])
    hid_grad[...] = jnp.zeros_like(hid_grad)

    def slope_step(at):
        cols = cols_at(at * COLS, COLS)
        slope_f[at] = gelu_slope(v_feat[:, cols].astype(f32))

    repeat(chunks, slope_step)

    def gather_step(at):
        swap_copy(at).wait_recv()
        where = rows_at(at * COLS, COLS)
        value = swap_out[at].astype(f32) + swap_in[at].astype(f32)
        out_grad[at] = value
        rounded = value.astype(bf16)
        hid_grad[...] += times(rounded, v_pw[where, :])
        early[0, where, :] = transposed_times(rounded, hidden[...]).astype(bf16)

    repeat(chunks, gather_step)
    mid_grad[...] = (hid_grad[...] * slope_m[...]).astype(bf16)
    ahead, behind = (mid_grad, earlier), (mid_grad, later)
    send_halo(z, y, ahead, behind, halo_s, halo_r)

    loads[4].wait()

    def centre_step(at):
        where = rows_at(at * rows, rows)
        early[1, where, :] = times(act_t[where, :], mid_grad[...]).astype(bf16)

    repeat(NZ, centre_step)
    order = (7, 1, 6, 2, 5, 3, 4, 0)

    def early_sibling(slot):
        where = rows_at(lax.rem(z + order[slot], NZ) * rows, rows)
        return remote(early.at[1 - c, where], sib_early.at[where], sibe_s.at[slot], sibe_r.at[slot], c=1 - c)

    for slot in range(NZ):
        early_sibling(slot).start()

    def partial(at, way, piece):
        where = rows_at(at * rows + (way * PIECES + piece) * sub, sub)
        return early[c, where, :].astype(f32) + sib_early[where, :].astype(f32)

    def ring_copy(step, way, piece):
        return remote(
            ring_out.at[step, way, piece], ring_in.at[step, way, piece],
            ring_s.at[step, way, piece], ring_r.at[step, way, piece], z=up if way == 0 else down,
        )

    def ring_step(step):
        for piece in range(PIECES):
            for way in range(HALVES):
                at = lax.rem(z + NZ - 1 - step, NZ) if way == 0 else lax.rem(z + 1 + step, NZ)
                value = partial(at, way, piece)
                if step:
                    ring_copy(step - 1, way, piece).wait_recv()
                    value = value + ring_in[step - 1, way, piece].astype(f32)
                ring_out[step, way, piece] = value.astype(bf16)
                ring_copy(step, way, piece).start()

    early_sibling(0).wait_recv()
    early_sibling(1).wait_recv()
    ring_step(0)
    for slot in range(2, NZ):
        early_sibling(slot).wait_recv()
    ring_step(1)
    ring_step(2)
    wait_halo(z, y, ahead, behind, halo_s, halo_r)

    def late_sibling(at):
        where = rows_at(at * rows, rows)
        return remote(late.at[1 - c, where], sib_late.at[where], sibl_s.at[at], sibl_r.at[at], c=1 - c)

    def late_step(turn):
        at = lax.rem(z + turn, NZ)
        where = rows_at(at * rows, rows)
        late[0, where, :] = times(act_t[where, :], later[...]).astype(bf16)
        late[1, where, :] = times(act_t[where, :], earlier[...]).astype(bf16)
        late_sibling(at).start()

    def y_copy(at, step):
        return remote(
            y_out.at[at, rows_at(lax.rem(y + step, NY) * part, part)], y_in.at[at, step - 1],
            y_s.at[at, step - 1], y_r.at[at, step - 1], y=lax.rem(y + step, NY),
        )

    def y_step(turn):
        at = lax.rem(z + turn, NZ)
        where = rows_at(at * rows, rows)
        late_sibling(at).wait_recv()
        y_out[at] = (late[c, where, :].astype(f32) + sib_late[where, :].astype(f32)).astype(bf16)
        for step in range(1, NY):
            y_copy(at, step).start()

    def late_and_y_step(turn):
        late_step(turn)
        y_step(turn - 1)

    late_step(1)
    repeat(NZ + 1, late_and_y_step, 2)
    y_step(NZ)
    ring_step(3)
    loads[5].wait()

    def act_copy(at):
        return remote(act_out.at[at], act_in.at[at], acts_s.at[at], acts_r.at[at], h=1 - h)

    def act_step(at):
        where = rows_at(at * COLS, COLS)
        value = times_transposed(later[...], v_w3[0, where, :])
        value = value + times_transposed(mid_grad[...], v_w3[1, where, :])
        value = value + times_transposed(earlier[...], v_w3[2, where, :])
        act_out[at] = value.astype(bf16)
        act_copy(at).start()

    repeat(chunks, act_step)
    ring_step(4)

    def z_copy(turn, at, twist):
        to = lax.rem(corner + twist, 4)
        return remote(
            z_out.at[at, to], z_in.at[z, corner], z_s.at[turn - 1, twist], z_r.at[turn - 1, twist],
            z=at, **corner_of(to),
        )

    def z_sum(turn):
        at = lax.rem(z + turn, NZ)
        where = rows_at(at * rows + y * part, part)
        value = late[c, where, :].astype(f32) + sib_late[where, :].astype(f32)
        for step in range(1, NY):
            y_copy(at, step).wait_recv()
            value = value + y_in[at, step - 1].astype(f32)
        z_tile[...] = value
        for to in range(4):
            z_out[at, to] = z_tile[to * each:(to + 1) * each, :].astype(bf16)
        return at

    def z_step(turn):
        at = z_sum(turn)
        for twist in range(4):
            z_copy(turn, at, twist).start()

    z_step(1)
    z_step(2)
    ring_step(5)
    z_step(3)
    z_step(4)
    ring_step(6)
    z_step(5)
    z_step(6)
    z_step(7)
    z_sum(NZ)
    for twist in range(1, 4):
        z_copy(NZ, z, twist).start()
    z_in[z, corner] = z_out[z, corner]

    for piece in range(PIECES):
        for way in range(HALVES):
            value = partial(z, way, piece)
            ring_copy(NZ - 2, way, piece).wait_recv()
            value = value + ring_in[NZ - 2, way, piece].astype(f32)
            final[(way * PIECES + piece) * sub:(way * PIECES + piece + 1) * sub, :] = value
    for at in range(16):
        early_out[at] = final[at * each:(at + 1) * each, :].astype(bf16)

    def fin_copy(step):
        to = lax.rem(me + step, 16)
        return remote(early_out.at[to], early_in.at[me], fin_s.at[step - 1], fin_r.at[step - 1], **group(to))

    for step in range(1, 16):
        fin_copy(step).start()
    early_in[me] = early_out[me]

    def out_step(at):
        act_copy(at).wait_recv()
        value = act_out[at].astype(f32) + act_in[at].astype(f32)
        grad_out[:, cols_at(at * COLS, COLS)] = (out_grad[at] + value * slope_f[at]).astype(bf16)

    repeat(chunks, out_step)
    for turn in range(1, NZ + 1):
        for twist in range(1 if turn == NZ else 0, 4):
            source = lax.rem(z + 2 * NZ - turn, NZ)
            ref = z_in.at[source, lax.rem(corner + 4 - twist, 4)]
            remote(ref, ref, z_s.at[turn - 1, twist], z_r.at[turn - 1, twist], z=z).wait_recv()
    for core in range(2):
        total = jnp.zeros((each, hidden.shape[1]), f32)
        for turn in range(NZ):
            for sample in range(2):
                total = total + z_in[turn, core * 2 + sample].astype(f32)
        summed[2 + core] = total
    for step in range(1, 16):
        ref = early_in.at[lax.rem(me + 16 - step, 16)]
        remote(ref, ref, fin_s.at[step - 1], fin_r.at[step - 1], z=z).wait_recv()
    for core in range(2):
        total = jnp.zeros((each, hidden.shape[1]), f32)
        for row in range(NY):
            for sample in range(2):
                total = total + early_in[(row * 2 + core) * 2 + sample].astype(f32)
        summed[core] = total

    def drain_chunks(at):
        swap_copy(at).wait_send()
        act_copy(at).wait_send()

    repeat(chunks, drain_chunks)
    drain_halo(z, y, ahead, behind, halo_s, halo_r)
    for slot in range(NZ):
        early_sibling(slot).wait_send()
    for step in range(NZ - 1):
        for piece in range(PIECES):
            for way in range(HALVES):
                ring_copy(step, way, piece).wait_send()

    def drain_late(at):
        late_sibling(at).wait_send()
        for step in range(1, NY):
            y_copy(at, step).wait_send()

    repeat(NZ, drain_late)
    for turn in range(1, NZ + 1):
        for twist in range(1 if turn == NZ else 0, 4):
            z_copy(turn, lax.rem(z + turn, NZ), twist).wait_send()
    for step in range(1, 16):
        fin_copy(step).wait_send()


def backward(feat, hidden, middle, block, act_t, tw, cot, pw, w3):
    bf16, f32 = jnp.bfloat16, jnp.float32
    positions, channels = feat.shape
    width = pw.shape[1]
    tracks = tw.shape[1]
    chunks = channels // COLS
    rows = channels // NZ
    part = rows // NY
    each = part // 4
    sub = rows // HALVES // PIECES
    ring = (NZ - 1, HALVES, PIECES)
    tile = (chunks, positions, COLS)
    return pl.pallas_call(
        backward_kernel,
        out_shape=(
            jax.ShapeDtypeStruct((positions, channels), bf16),
            jax.ShapeDtypeStruct((4, each, width), f32),
        ),
        in_specs=[ANY, VMEM, VMEM, ANY, ANY, ANY, ANY, ANY, ANY],
        out_specs=(VMEM, VMEM),
        scratch_shapes=[
            pltpu.VMEM(feat.shape, bf16),
            pltpu.VMEM(feat.shape, bf16),
            pltpu.VMEM(act_t.shape, bf16),
            pltpu.VMEM(tw.shape, bf16),
            pltpu.VMEM(cot.shape, bf16),
            pltpu.VMEM(pw.shape, bf16),
            pltpu.VMEM(w3.shape, bf16),
            pltpu.VMEM((positions, tracks), bf16),
            pltpu.VMEM(tile, f32),
            pltpu.VMEM(tile, f32),
            pltpu.VMEM((positions, width), f32),
            pltpu.VMEM((positions, width), f32),
            pltpu.VMEM((positions, width), bf16),
            pltpu.VMEM((positions, width), bf16),
            pltpu.VMEM((positions, width), bf16),
            pltpu.VMEM(tile, bf16),
            pltpu.VMEM(tile, bf16),
            pltpu.VMEM(tile, bf16),
            pltpu.VMEM(tile, bf16),
            pltpu.VMEM((2, channels, width), bf16),
            pltpu.VMEM((2, channels, width), bf16),
            pltpu.VMEM((channels, width), bf16),
            pltpu.VMEM((channels, width), bf16),
            pltpu.VMEM((*ring, sub, width), bf16),
            pltpu.VMEM((*ring, sub, width), bf16),
            pltpu.VMEM((rows, width), f32),
            pltpu.VMEM((16, each, width), bf16),
            pltpu.VMEM((16, each, width), bf16),
            pltpu.VMEM((NZ, rows, width), bf16),
            pltpu.VMEM((NZ, NY - 1, part, width), bf16),
            pltpu.VMEM((part, width), f32),
            pltpu.VMEM((NZ, 4, each, width), bf16),
            pltpu.VMEM((NZ, 4, each, width), bf16),
            DMA((6,)), DMA((tracks // COLS + 1,)),
            DMA((chunks,)), DMA((chunks,)),
            DMA((chunks,)), DMA((chunks,)),
            DMA((2,)), DMA((2,)),
            DMA((NZ,)), DMA((NZ,)),
            DMA((NZ,)), DMA((NZ,)),
            DMA(ring), DMA(ring),
            DMA((15,)), DMA((15,)),
            DMA((NZ, NY - 1)), DMA((NZ, NY - 1)),
            DMA((NZ, 4)), DMA((NZ, 4)),
        ],
        compiler_params=pltpu.CompilerParams(
            collective_id=1, has_side_effects=True, vmem_limit_bytes=60000000
        ),
        name="backward",
    )(feat, hidden, middle, block, act_t, tw, cot, pw, w3)


def body(features, dilated_weight, point_weight, track_weight, track_cotangent):
    samples, positions, channels = features.shape
    number_rows = samples * positions
    feat = features.reshape(number_rows, channels)
    taps_weight = jnp.transpose(dilated_weight, (1, 0, 2))
    middle, hidden, block, turned, whole_track = forward_exchange(
        feat, taps_weight, track_weight, point_weight
    )
    whole_track = whole_track.reshape(channels, track_weight.shape[1])
    cotangent = track_cotangent.reshape(number_rows, whole_track.shape[1])
    input_grad, summed = backward(
        feat, hidden, middle, block, turned, whole_track, cotangent, point_weight, taps_weight
    )
    dilated_grad = jnp.stack([summed[2], summed[1], summed[3]], axis=1)
    return (input_grad.reshape(samples, positions, channels), dilated_grad, summed[0])


def solution(mesh):
    torus = Mesh(
        mesh.devices.reshape(NZ, NY, 2, mesh.shape["head"], mesh.shape["sample"]),
        ("z", "y", "c", "h", "s"),
    )
    placed = (
        P("s", SEQ, None),
        P(None, None, "h"),
        P(None, "h"),
        P("s", "h"),
        P("s", SEQ, "h"),
    )
    return jax.shard_map(
        body,
        mesh=torus,
        in_specs=placed,
        out_specs=(P("s", SEQ, None), P(SEQ_SAMPLE, None, "h"), P(SEQ_SAMPLE, "h")),
        check_vma=False,
    )
```

```python
import jax
import jax.numpy as jnp
from jax import lax
from jax.experimental import pallas as pl
from jax.experimental.pallas import tpu as pltpu
from jax.sharding import Mesh
from jax.sharding import PartitionSpec as P

MESH = pl.DeviceIdType.MESH
SEQ = ("z", "y", "c")
SEQ_SAMPLE = ("z", "y", "c", "s")
NZ, NY = 8, 4
VMEM = pl.BlockSpec(memory_space=pltpu.VMEM)
ANY = pl.BlockSpec(memory_space=pltpu.HBM)
DMA = pltpu.SemaphoreType.DMA


def gelu_value(value):
    inner = 0.7978845608 * (value + 0.044715 * value * value * value)
    return 0.5 * value * (1.0 + jnp.tanh(inner))


def gelu_slope(value):
    inner = 0.7978845608 * (value + 0.044715 * value * value * value)
    tangent = jnp.tanh(inner)
    return 0.5 * (1.0 + tangent) + 0.5 * value * (1.0 - tangent * tangent) * 0.7978845608 * (
        1.0 + 3.0 * 0.044715 * value * value
    )


def times(left, right):
    return jnp.dot(left, right, preferred_element_type=jnp.float32)


def times_transposed(left, right):
    return lax.dot_general(
        left, right, (((1,), (1,)), ((), ())), preferred_element_type=jnp.float32
    )


def transposed_times(left, right):
    return lax.dot_general(
        left, right, (((0,), (0,)), ((), ())), preferred_element_type=jnp.float32
    )


def place():
    return tuple(lax.axis_index(name) for name in ("z", "y", "c", "h", "s"))


def remote(source, target, sent, arrived, **device):
    return pltpu.make_async_remote_copy(
        src_ref=source,
        dst_ref=target,
        send_sem=sent,
        recv_sem=arrived,
        device_id=device,
        device_id_type=MESH,
    )


def greet(barrier, **device):
    pl.semaphore_signal(barrier, inc=1, device_id=device, device_id_type=MESH)


def rows_at(start, size):
    return pl.ds(pl.multiple_of(start, 16), size)


def shifted(z, y, step):
    at = z * NY + y + step
    return {"z": lax.div(at, NY), "y": lax.rem(at, NY)}


def has_neighbours(z, y):
    at = z * NY + y
    return at >= 2, at < NZ * NY - 2


def send_halo(z, y, ahead, behind, sent, arrived):
    before, after = has_neighbours(z, y)

    @pl.when(after)
    def _():
        remote(*ahead, sent.at[0], arrived.at[0], **shifted(z, y, 2)).start()

    @pl.when(before)
    def _():
        remote(*behind, sent.at[1], arrived.at[1], **shifted(z, y, -2)).start()


def wait_halo(z, y, ahead, behind, sent, arrived):
    before, after = has_neighbours(z, y)

    @pl.when(before)
    def _():
        remote(*ahead, sent.at[0], arrived.at[0], c=lax.axis_index("c")).wait_recv()

    @pl.when(jnp.logical_not(before))
    def _():
        ahead[1][...] = jnp.zeros_like(ahead[1])

    @pl.when(after)
    def _():
        remote(*behind, sent.at[1], arrived.at[1], c=lax.axis_index("c")).wait_recv()

    @pl.when(jnp.logical_not(after))
    def _():
        behind[1][...] = jnp.zeros_like(behind[1])


def drain_halo(z, y, ahead, behind, sent, arrived):
    before, after = has_neighbours(z, y)

    @pl.when(after)
    def _():
        remote(*ahead, sent.at[0], arrived.at[0], c=lax.axis_index("c")).wait_send()

    @pl.when(before)
    def _():
        remote(*behind, sent.at[1], arrived.at[1], c=lax.axis_index("c")).wait_send()


def greet_halo(barrier, z, y):
    before, after = has_neighbours(z, y)

    @pl.when(after)
    def _():
        greet(barrier, **shifted(z, y, 2))

    @pl.when(before)
    def _():
        greet(barrier, **shifted(z, y, -2))

    return before.astype(jnp.int32) + after.astype(jnp.int32)


COLS = 256
HALVES, PIECES = 2, 2


def cols_at(start, size):
    return pl.ds(pl.multiple_of(start, 128), size)


def repeat(count, step, start=0):
    def once(at, carry):
        step(at)
        return carry

    lax.fori_loop(start, count, once, 0)


YROWS, ZROWS, ZCUT = 40, 56, 32


def forward_kernel(
    feat, w3, tw, pw, middle, hid_own, block, act_t, twf,
    v_feat, v_w3, v_pw, own, act, ahead_out, behind_out, from_before, from_after, centre, hid_other, pwo,
    load, own_sem, halo_s, halo_r, hid_s, hid_r, x_s, x_r, y_s, y_r, pz_s, pz_r, tz_s, tz_r, sib_s, sib_r,
):
    z, y, c, h, s = place()
    bf16, f32 = jnp.bfloat16, jnp.float32
    channels = feat.shape[1]
    chunks = channels // COLS
    barrier = pltpu.get_barrier_semaphore()
    greet(barrier, h=1 - h)
    greet(barrier, s=1 - s)
    greet(barrier, c=1 - c)
    for step in (1, 2, NZ - 2, NZ - 1):
        greet(barrier, z=lax.rem(z + step, NZ))
    for step in range(1, NY):
        greet(barrier, y=lax.rem(y + step, NY))
    greeted = 10 + greet_halo(barrier, z, y)
    loads = [
        pltpu.make_async_copy(source, target, load.at[slot])
        for slot, (source, target) in enumerate(
            ((feat, v_feat), (w3.at[0], v_w3.at[0]), (w3.at[2], v_w3.at[2]), (w3.at[1], v_w3.at[1]), (pw, v_pw))
        )
    ]
    for copy in loads:
        copy.start()
    take_own = pltpu.make_async_copy(tw, own, own_sem.at[0])
    take_own.start()

    half = tw.shape[0] // 2
    point = pw.shape[0] // 2
    p_rows = point // 4
    other = 1 - s

    def rows8(start, size):
        return pl.ds(pl.multiple_of(start, 8), size)

    def y_rows(core, at):
        return rows8(core * half + at * YROWS, YROWS)

    def z_rows(core, at, cut):
        start = core * half + NY * YROWS + lax.rem(at, 4) * ZROWS
        return rows8(start, ZCUT) if cut == 0 else rows8(start + ZCUT, ZROWS - ZCUT)

    def p_rows_of(core, at, cut):
        start = core * point + lax.rem(at, 4) * p_rows
        if cut is None:
            return rows8(start, p_rows)
        return rows8(start + cut * (p_rows // 2), p_rows // 2)

    started = []

    def go(ref, target, sent, arrived, **device):
        copy = remote(ref, target, sent, arrived, **device)
        copy.start()
        started.append(copy)

    def landing(ref, sent, arrived):
        remote(ref, ref, sent, arrived, c=1 - c).wait_recv()

    pl.semaphore_wait(barrier, greeted)
    here = p_rows_of(c, z, None)
    go(pw.at[here], pwo.at[here], x_s.at[0], x_r.at[0], h=1 - h)
    for cut in range(2):
        here = z_rows(c, z, cut)
        go(tw.at[here], twf.at[s, here], x_s.at[1 + cut], x_r.at[1 + cut], s=1 - s)
    here = y_rows(c, y)
    go(tw.at[here], twf.at[s, here], x_s.at[3], x_r.at[3], s=1 - s)

    loads[0].wait()

    def act_step(at):
        cols = cols_at(at * COLS, COLS)
        act[:, cols] = gelu_value(v_feat[:, cols].astype(f32)).astype(bf16)

    repeat(chunks, act_step)
    before, after = has_neighbours(z, y)
    ahead, behind = (ahead_out, from_before), (behind_out, from_after)
    loads[1].wait()
    ahead_out[...] = times(act[...], v_w3[0]).astype(bf16)

    @pl.when(after)
    def _():
        remote(*ahead, halo_s.at[0], halo_r.at[0], **shifted(z, y, 2)).start()

    loads[2].wait()
    behind_out[...] = times(act[...], v_w3[2]).astype(bf16)

    @pl.when(before)
    def _():
        remote(*behind, halo_s.at[1], halo_r.at[1], **shifted(z, y, -2)).start()

    steps = (1, NZ - 1, 2, NZ - 2)
    here = pwo.at[p_rows_of(c, z, None)]
    landing(here, x_s.at[0], x_r.at[0])
    for slot in range(2):
        go(here, here, pz_s.at[slot], pz_r.at[slot], z=lax.rem(z + steps[slot], NZ))
    for cut in range(2):
        piece = pwo.at[p_rows_of(c, z, cut)]
        go(piece, piece, pz_s.at[2 + cut], pz_r.at[2 + cut], z=lax.rem(z + steps[2 + cut], NZ))
    go(here, here, sib_s.at[0], sib_r.at[0], c=1 - c)
    for cut in range(2):
        here = twf.at[other, z_rows(c, z, cut)]
        landing(here, x_s.at[1 + cut], x_r.at[1 + cut])
        for slot, step in enumerate((steps[0], steps[1], steps[2 + cut])):
            go(here, here, tz_s.at[cut, slot], tz_r.at[cut, slot], z=lax.rem(z + step, NZ))
        go(here, here, sib_s.at[5 + cut], sib_r.at[5 + cut], c=1 - c)
        if cut == 0:
            loads[3].wait()
            centre[...] = times(act[...], v_w3[1])
    here = twf.at[other, y_rows(c, y)]
    landing(here, x_s.at[3], x_r.at[3])
    for step in range(1, NY):
        go(here, here, y_s.at[step - 1], y_r.at[step - 1], y=lax.rem(y + step, NY))
    go(here, here, sib_s.at[13], sib_r.at[13], c=1 - c)
    take_own.wait()
    put_own = pltpu.make_async_copy(own, twf.at[s], own_sem.at[1])
    put_own.start()

    def turn_step(at):
        act_t[rows_at(at * COLS, COLS), :] = act[:, cols_at(at * COLS, COLS)].T

    repeat(chunks, turn_step)

    def p_from(core, slot):
        at = z + NZ - steps[slot]
        return pwo.at[p_rows_of(core, at, None if slot < 2 else slot - 2)]

    def t_from(core, cut, slot):
        step = steps[slot] if slot < 2 else steps[2 + cut]
        return twf.at[other, z_rows(core, z + NZ - step, cut)]

    def y_from(core, step):
        return twf.at[other, y_rows(core, lax.rem(y + NY - step, NY))]

    for slot in range(4):
        here = p_from(c, slot)
        landing(here, pz_s.at[slot], pz_r.at[slot])
        go(here, here, sib_s.at[1 + slot], sib_r.at[1 + slot], c=1 - c)

    wait_halo(z, y, ahead, behind, halo_s, halo_r)
    total = centre[...] + from_before[...].astype(f32) + from_after[...].astype(f32)
    middle[...] = total
    hid_own[...] = gelu_value(total).astype(bf16)
    go(hid_own, hid_other, hid_s, hid_r, h=1 - h)

    for cut in range(2):
        for slot in range(3):
            here = t_from(c, cut, slot)
            landing(here, tz_s.at[cut, slot], tz_r.at[cut, slot])
            at = 7 + cut * 3 + slot
            go(here, here, sib_s.at[at], sib_r.at[at], c=1 - c)
    for step in range(1, NY):
        here = y_from(c, step)
        landing(here, y_s.at[step - 1], y_r.at[step - 1])
        go(here, here, sib_s.at[13 + step], sib_r.at[13 + step], c=1 - c)

    landing(pwo.at[p_rows_of(1 - c, z, None)], sib_s.at[0], sib_r.at[0])
    for slot in range(4):
        landing(p_from(1 - c, slot), sib_s.at[1 + slot], sib_r.at[1 + slot])
    loads[4].wait()
    landing(hid_other, hid_s, hid_r)

    def block_step(at):
        cols, where = cols_at(at * COLS, COLS), rows_at(at * COLS, COLS)
        value = v_feat[:, cols].astype(f32)
        value = value + times_transposed(hid_own[...], v_pw[where, :])
        value = value + times_transposed(hid_other[...], pwo[where, :])
        block[:, cols] = value.astype(bf16)

    repeat(chunks, block_step)
    for cut in range(2):
        landing(twf.at[other, z_rows(1 - c, z, cut)], sib_s.at[5 + cut], sib_r.at[5 + cut])
        for slot in range(3):
            at = 7 + cut * 3 + slot
            landing(t_from(1 - c, cut, slot), sib_s.at[at], sib_r.at[at])
    landing(twf.at[other, y_rows(1 - c, y)], sib_s.at[13], sib_r.at[13])
    for step in range(1, NY):
        landing(y_from(1 - c, step), sib_s.at[13 + step], sib_r.at[13 + step])
    for copy in started:
        copy.wait_send()
    drain_halo(z, y, ahead, behind, halo_s, halo_r)
    put_own.wait()


def forward_exchange(feat, w3, tw, pw):
    bf16, f32 = jnp.bfloat16, jnp.float32
    positions, channels = feat.shape
    width = pw.shape[1]
    return pl.pallas_call(
        forward_kernel,
        out_shape=(
            jax.ShapeDtypeStruct((positions, width), f32),
            jax.ShapeDtypeStruct((positions, width), bf16),
            jax.ShapeDtypeStruct((positions, channels), bf16),
            jax.ShapeDtypeStruct((channels, positions), bf16),
            jax.ShapeDtypeStruct((2, *tw.shape), bf16),
        ),
        in_specs=[ANY, ANY, ANY, ANY],
        out_specs=(VMEM, VMEM, VMEM, VMEM, ANY),
        scratch_shapes=[
            pltpu.VMEM(feat.shape, bf16),
            pltpu.VMEM(w3.shape, bf16),
            pltpu.VMEM(pw.shape, bf16),
            pltpu.VMEM(tw.shape, bf16),
            pltpu.VMEM(feat.shape, bf16),
            pltpu.VMEM((positions, width), bf16),
            pltpu.VMEM((positions, width), bf16),
            pltpu.VMEM((positions, width), bf16),
            pltpu.VMEM((positions, width), bf16),
            pltpu.VMEM((positions, width), f32),
            pltpu.VMEM((positions, width), bf16),
            pltpu.VMEM(pw.shape, bf16),
            DMA((5,)), DMA((2,)),
            DMA((2,)), DMA((2,)),
            DMA, DMA,
            DMA((4,)), DMA((4,)),
            DMA((3,)), DMA((3,)),
            DMA((4,)), DMA((4,)),
            DMA((2, 3)), DMA((2, 3)),
            DMA((17,)), DMA((17,)),
        ],
        compiler_params=pltpu.CompilerParams(
            collective_id=0, has_side_effects=True, vmem_limit_bytes=67043328
        ),
        name="forward_exchange",
    )(feat, w3, tw, pw)


def backward_kernel(
    feat, hidden, middle, block_hbm, act_hbm, tw, cot, pw, w3, grad_out, summed,
    v_feat, block, act_t, v_tw, v_cot, v_pw, v_w3, score, out_grad, slope_f, slope_m,
    hid_grad, mid_grad, later, earlier, swap_out, swap_in, act_out, act_in,
    early, late, sib_early, sib_late, ring_out, ring_in, final, early_out, early_in,
    y_out, y_in, z_tile, z_out, z_in,
    load, tw_load, swap_s, swap_r, acts_s, acts_r, halo_s, halo_r, sibe_s, sibe_r, sibl_s, sibl_r,
    ring_s, ring_r, fin_s, fin_r, y_s, y_r, z_s, z_r,
):
    z, y, c, h, s = place()
    up, down = lax.rem(z + 1, NZ), lax.rem(z + NZ - 1, NZ)
    me = (y * 2 + c) * 2 + s
    corner = c * 2 + s
    channels, tracks = tw.shape
    chunks = channels // COLS
    rows = channels // NZ
    part = rows // NY
    each = part // 4
    sub = rows // HALVES // PIECES
    bf16, f32 = jnp.bfloat16, jnp.float32

    def group(at):
        return {"y": lax.div(at, 4), "c": lax.rem(lax.div(at, 2), 2), "s": lax.rem(at, 2)}

    def corner_of(at):
        return {"c": lax.div(at, 2), "s": lax.rem(at, 2)}

    barrier = pltpu.get_barrier_semaphore()
    greet(barrier, h=1 - h)
    for step in range(1, 16):
        greet(barrier, **group(lax.rem(me + step, 16)))
    for step in range(1, NZ):
        for turn in range(4):
            greet(barrier, z=lax.rem(z + step, NZ), **corner_of(turn))
    greeted = 1 + 15 + 4 * (NZ - 1) + greet_halo(barrier, z, y)

    loads = [
        pltpu.make_async_copy(source, target, load.at[slot])
        for slot, (source, target) in enumerate(
            ((block_hbm, block), (cot, v_cot), (feat, v_feat), (pw, v_pw), (act_hbm, act_t), (w3, v_w3))
        )
    ]
    whole, tail = tracks // COLS, tracks % COLS

    def tw_copy(at, size=COLS):
        where = cols_at(at * COLS, size)
        return pltpu.make_async_copy(tw.at[:, where], v_tw.at[:, where], tw_load.at[at])

    loads[0].start()
    repeat(whole, lambda at: tw_copy(at).start())
    tw_copy(whole, tail).start()
    for copy in loads[1:]:
        copy.start()
    loads[0].wait()
    loads[1].wait()

    def score_step(at, size=COLS):
        tw_copy(at, size).wait()
        cols = cols_at(at * COLS, size)
        value = jax.nn.sigmoid(times(block[...], v_tw[:, cols]))
        score[:, cols] = (v_cot[:, cols].astype(f32) * value).astype(bf16)

    repeat(whole, score_step)
    score_step(whole, tail)
    pl.semaphore_wait(barrier, greeted)

    def swap_copy(at):
        return remote(swap_out.at[at], swap_in.at[at], swap_s.at[at], swap_r.at[at], h=1 - h)

    def swap_step(at):
        swap_out[at] = times_transposed(score[...], v_tw[rows_at(at * COLS, COLS), :]).astype(bf16)
        swap_copy(at).start()

    repeat(chunks, swap_step)
    loads[2].wait()
    loads[3].wait()
    slope_m[...] = gelu_slope(middle[...])
    hid_grad[...] = jnp.zeros_like(hid_grad)

    def slope_step(at):
        cols = cols_at(at * COLS, COLS)
        slope_f[at] = gelu_slope(v_feat[:, cols].astype(f32))

    repeat(chunks, slope_step)

    def gather_step(at):
        swap_copy(at).wait_recv()
        where = rows_at(at * COLS, COLS)
        value = swap_out[at].astype(f32) + swap_in[at].astype(f32)
        out_grad[at] = value
        rounded = value.astype(bf16)
        hid_grad[...] += times(rounded, v_pw[where, :])
        early[0, where, :] = transposed_times(rounded, hidden[...]).astype(bf16)

    repeat(chunks, gather_step)
    mid_grad[...] = (hid_grad[...] * slope_m[...]).astype(bf16)
    ahead, behind = (mid_grad, earlier), (mid_grad, later)
    send_halo(z, y, ahead, behind, halo_s, halo_r)

    loads[4].wait()

    def centre_step(at):
        where = rows_at(at * rows, rows)
        early[1, where, :] = times(act_t[where, :], mid_grad[...]).astype(bf16)

    repeat(NZ, centre_step)
    order = (7, 1, 6, 2, 5, 3, 4, 0)

    def early_sibling(slot):
        where = rows_at(lax.rem(z + order[slot], NZ) * rows, rows)
        return remote(early.at[1 - c, where], sib_early.at[where], sibe_s.at[slot], sibe_r.at[slot], c=1 - c)

    for slot in range(NZ):
        early_sibling(slot).start()

    def partial(at, way, piece):
        where = rows_at(at * rows + (way * PIECES + piece) * sub, sub)
        return early[c, where, :].astype(f32) + sib_early[where, :].astype(f32)

    def ring_copy(step, way, piece):
        return remote(
            ring_out.at[step, way, piece], ring_in.at[step, way, piece],
            ring_s.at[step, way, piece], ring_r.at[step, way, piece], z=up if way == 0 else down,
        )

    def ring_step(step):
        for piece in range(PIECES):
            for way in range(HALVES):
                at = lax.rem(z + NZ - 1 - step, NZ) if way == 0 else lax.rem(z + 1 + step, NZ)
                value = partial(at, way, piece)
                if step:
                    ring_copy(step - 1, way, piece).wait_recv()
                    value = value + ring_in[step - 1, way, piece].astype(f32)
                ring_out[step, way, piece] = value.astype(bf16)
                ring_copy(step, way, piece).start()

    early_sibling(0).wait_recv()
    early_sibling(1).wait_recv()
    ring_step(0)
    for slot in range(2, NZ):
        early_sibling(slot).wait_recv()
    ring_step(1)
    ring_step(2)
    wait_halo(z, y, ahead, behind, halo_s, halo_r)

    def late_sibling(at):
        where = rows_at(at * rows, rows)
        return remote(late.at[1 - c, where], sib_late.at[where], sibl_s.at[at], sibl_r.at[at], c=1 - c)

    def late_step(turn):
        at = lax.rem(z + turn, NZ)
        where = rows_at(at * rows, rows)
        late[0, where, :] = times(act_t[where, :], later[...]).astype(bf16)
        late[1, where, :] = times(act_t[where, :], earlier[...]).astype(bf16)
        late_sibling(at).start()

    def y_copy(at, step):
        return remote(
            y_out.at[at, rows_at(lax.rem(y + step, NY) * part, part)], y_in.at[at, step - 1],
            y_s.at[at, step - 1], y_r.at[at, step - 1], y=lax.rem(y + step, NY),
        )

    def y_step(turn):
        at = lax.rem(z + turn, NZ)
        where = rows_at(at * rows, rows)
        late_sibling(at).wait_recv()
        y_out[at] = (late[c, where, :].astype(f32) + sib_late[where, :].astype(f32)).astype(bf16)
        for step in range(1, NY):
            y_copy(at, step).start()

    def act_copy(at):
        return remote(act_out.at[at], act_in.at[at], acts_s.at[at], acts_r.at[at], h=1 - h)

    def act_step(at):
        where = rows_at(at * COLS, COLS)
        value = times_transposed(later[...], v_w3[0, where, :])
        value = value + times_transposed(mid_grad[...], v_w3[1, where, :])
        value = value + times_transposed(earlier[...], v_w3[2, where, :])
        act_out[at] = value.astype(bf16)
        act_copy(at).start()

    def mixed_step(turn):
        act_step(turn - 1)
        late_step(turn + 1)
        y_step(turn)

    loads[5].wait()
    late_step(1)
    repeat(chunks // 2 + 1, mixed_step, 1)
    ring_step(3)
    repeat(chunks + 1, mixed_step, chunks // 2 + 1)
    ring_step(4)
    late_step(NZ)
    y_step(NZ - 1)
    y_step(NZ)

    def z_copy(turn, at, twist):
        to = lax.rem(corner + twist, 4)
        return remote(
            z_out.at[at, to], z_in.at[z, corner], z_s.at[turn - 1, twist], z_r.at[turn - 1, twist],
            z=at, **corner_of(to),
        )

    def z_sum(turn):
        at = lax.rem(z + turn, NZ)
        where = rows_at(at * rows + y * part, part)
        value = late[c, where, :].astype(f32) + sib_late[where, :].astype(f32)
        for step in range(1, NY):
            y_copy(at, step).wait_recv()
            value = value + y_in[at, step - 1].astype(f32)
        z_tile[...] = value
        for to in range(4):
            z_out[at, to] = z_tile[to * each:(to + 1) * each, :].astype(bf16)
        return at

    def z_step(turn):
        at = z_sum(turn)
        for twist in range(4):
            z_copy(turn, at, twist).start()

    z_step(1)
    z_step(2)
    ring_step(5)
    z_step(3)
    z_step(4)
    ring_step(6)
    z_step(5)
    z_step(6)
    z_step(7)
    z_sum(NZ)
    for twist in range(1, 4):
        z_copy(NZ, z, twist).start()
    z_in[z, corner] = z_out[z, corner]

    for piece in range(PIECES):
        for way in range(HALVES):
            value = partial(z, way, piece)
            ring_copy(NZ - 2, way, piece).wait_recv()
            value = value + ring_in[NZ - 2, way, piece].astype(f32)
            final[(way * PIECES + piece) * sub:(way * PIECES + piece + 1) * sub, :] = value
    for at in range(16):
        early_out[at] = final[at * each:(at + 1) * each, :].astype(bf16)

    def fin_copy(step):
        to = lax.rem(me + step, 16)
        return remote(early_out.at[to], early_in.at[me], fin_s.at[step - 1], fin_r.at[step - 1], **group(to))

    for step in range(1, 16):
        fin_copy(step).start()
    early_in[me] = early_out[me]

    def out_step(at):
        act_copy(at).wait_recv()
        value = act_out[at].astype(f32) + act_in[at].astype(f32)
        grad_out[:, cols_at(at * COLS, COLS)] = (out_grad[at] + value * slope_f[at]).astype(bf16)

    repeat(chunks, out_step)
    for turn in range(1, NZ + 1):
        for twist in range(1 if turn == NZ else 0, 4):
            source = lax.rem(z + 2 * NZ - turn, NZ)
            ref = z_in.at[source, lax.rem(corner + 4 - twist, 4)]
            remote(ref, ref, z_s.at[turn - 1, twist], z_r.at[turn - 1, twist], z=z).wait_recv()
    for core in range(2):
        total = jnp.zeros((each, hidden.shape[1]), f32)
        for turn in range(NZ):
            for sample in range(2):
                total = total + z_in[turn, core * 2 + sample].astype(f32)
        summed[2 + core] = total
    for step in range(1, 16):
        ref = early_in.at[lax.rem(me + 16 - step, 16)]
        remote(ref, ref, fin_s.at[step - 1], fin_r.at[step - 1], z=z).wait_recv()
    for core in range(2):
        total = jnp.zeros((each, hidden.shape[1]), f32)
        for row in range(NY):
            for sample in range(2):
                total = total + early_in[(row * 2 + core) * 2 + sample].astype(f32)
        summed[core] = total

    def drain_chunks(at):
        swap_copy(at).wait_send()
        act_copy(at).wait_send()

    repeat(chunks, drain_chunks)
    drain_halo(z, y, ahead, behind, halo_s, halo_r)
    for slot in range(NZ):
        early_sibling(slot).wait_send()
    for step in range(NZ - 1):
        for piece in range(PIECES):
            for way in range(HALVES):
                ring_copy(step, way, piece).wait_send()

    def drain_late(at):
        late_sibling(at).wait_send()
        for step in range(1, NY):
            y_copy(at, step).wait_send()

    repeat(NZ, drain_late)
    for turn in range(1, NZ + 1):
        for twist in range(1 if turn == NZ else 0, 4):
            z_copy(turn, lax.rem(z + turn, NZ), twist).wait_send()
    for step in range(1, 16):
        fin_copy(step).wait_send()


def backward(feat, hidden, middle, block, act_t, tw, cot, pw, w3):
    bf16, f32 = jnp.bfloat16, jnp.float32
    positions, channels = feat.shape
    width = pw.shape[1]
    tracks = tw.shape[1]
    chunks = channels // COLS
    rows = channels // NZ
    part = rows // NY
    each = part // 4
    sub = rows // HALVES // PIECES
    ring = (NZ - 1, HALVES, PIECES)
    tile = (chunks, positions, COLS)
    return pl.pallas_call(
        backward_kernel,
        out_shape=(
            jax.ShapeDtypeStruct((positions, channels), bf16),
            jax.ShapeDtypeStruct((4, each, width), f32),
        ),
        in_specs=[ANY, VMEM, VMEM, ANY, ANY, ANY, ANY, ANY, ANY],
        out_specs=(VMEM, VMEM),
        scratch_shapes=[
            pltpu.VMEM(feat.shape, bf16),
            pltpu.VMEM(feat.shape, bf16),
            pltpu.VMEM(act_t.shape, bf16),
            pltpu.VMEM(tw.shape, bf16),
            pltpu.VMEM(cot.shape, bf16),
            pltpu.VMEM(pw.shape, bf16),
            pltpu.VMEM(w3.shape, bf16),
            pltpu.VMEM((positions, tracks), bf16),
            pltpu.VMEM(tile, f32),
            pltpu.VMEM(tile, f32),
            pltpu.VMEM((positions, width), f32),
            pltpu.VMEM((positions, width), f32),
            pltpu.VMEM((positions, width), bf16),
            pltpu.VMEM((positions, width), bf16),
            pltpu.VMEM((positions, width), bf16),
            pltpu.VMEM(tile, bf16),
            pltpu.VMEM(tile, bf16),
            pltpu.VMEM(tile, bf16),
            pltpu.VMEM(tile, bf16),
            pltpu.VMEM((2, channels, width), bf16),
            pltpu.VMEM((2, channels, width), bf16),
            pltpu.VMEM((channels, width), bf16),
            pltpu.VMEM((channels, width), bf16),
            pltpu.VMEM((*ring, sub, width), bf16),
            pltpu.VMEM((*ring, sub, width), bf16),
            pltpu.VMEM((rows, width), f32),
            pltpu.VMEM((16, each, width), bf16),
            pltpu.VMEM((16, each, width), bf16),
            pltpu.VMEM((NZ, rows, width), bf16),
            pltpu.VMEM((NZ, NY - 1, part, width), bf16),
            pltpu.VMEM((part, width), f32),
            pltpu.VMEM((NZ, 4, each, width), bf16),
            pltpu.VMEM((NZ, 4, each, width), bf16),
            DMA((6,)), DMA((tracks // COLS + 1,)),
            DMA((chunks,)), DMA((chunks,)),
            DMA((chunks,)), DMA((chunks,)),
            DMA((2,)), DMA((2,)),
            DMA((NZ,)), DMA((NZ,)),
            DMA((NZ,)), DMA((NZ,)),
            DMA(ring), DMA(ring),
            DMA((15,)), DMA((15,)),
            DMA((NZ, NY - 1)), DMA((NZ, NY - 1)),
            DMA((NZ, 4)), DMA((NZ, 4)),
        ],
        compiler_params=pltpu.CompilerParams(
            collective_id=1, has_side_effects=True, vmem_limit_bytes=60000000
        ),
        name="backward",
    )(feat, hidden, middle, block, act_t, tw, cot, pw, w3)


def body(features, dilated_weight, point_weight, track_weight, track_cotangent):
    samples, positions, channels = features.shape
    number_rows = samples * positions
    feat = features.reshape(number_rows, channels)
    taps_weight = jnp.transpose(dilated_weight, (1, 0, 2))
    middle, hidden, block, turned, whole_track = forward_exchange(
        feat, taps_weight, track_weight, point_weight
    )
    whole_track = whole_track.reshape(channels, track_weight.shape[1])
    cotangent = track_cotangent.reshape(number_rows, whole_track.shape[1])
    input_grad, summed = backward(
        feat, hidden, middle, block, turned, whole_track, cotangent, point_weight, taps_weight
    )
    dilated_grad = jnp.stack([summed[2], summed[1], summed[3]], axis=1)
    return (input_grad.reshape(samples, positions, channels), dilated_grad, summed[0])


def solution(mesh):
    torus = Mesh(
        mesh.devices.reshape(NZ, NY, 2, mesh.shape["head"], mesh.shape["sample"]),
        ("z", "y", "c", "h", "s"),
    )
    placed = (
        P("s", SEQ, None),
        P(None, None, "h"),
        P(None, "h"),
        P("s", "h"),
        P("s", SEQ, "h"),
    )
    return jax.shard_map(
        body,
        mesh=torus,
        in_specs=placed,
        out_specs=(P("s", SEQ, None), P(SEQ_SAMPLE, None, "h"), P(SEQ_SAMPLE, "h")),
        check_vma=False,
    )
```

```python
import jax
import jax.numpy as jnp
from jax import lax
from jax.experimental import pallas as pl
from jax.experimental.pallas import tpu as pltpu
from jax.sharding import Mesh
from jax.sharding import PartitionSpec as P

MESH = pl.DeviceIdType.MESH
SEQ = ("z", "y", "c")
SEQ_SAMPLE = ("z", "y", "c", "s")
NZ, NY = 8, 4
VMEM = pl.BlockSpec(memory_space=pltpu.VMEM)
ANY = pl.BlockSpec(memory_space=pltpu.HBM)
DMA = pltpu.SemaphoreType.DMA


def gelu_value(value):
    inner = 0.7978845608 * (value + 0.044715 * value * value * value)
    return 0.5 * value * (1.0 + jnp.tanh(inner))


def gelu_slope(value):
    inner = 0.7978845608 * (value + 0.044715 * value * value * value)
    tangent = jnp.tanh(inner)
    return 0.5 * (1.0 + tangent) + 0.5 * value * (1.0 - tangent * tangent) * 0.7978845608 * (
        1.0 + 3.0 * 0.044715 * value * value
    )


def times(left, right):
    return jnp.dot(left, right, preferred_element_type=jnp.float32)


def times_transposed(left, right):
    return lax.dot_general(
        left, right, (((1,), (1,)), ((), ())), preferred_element_type=jnp.float32
    )


def transposed_times(left, right):
    return lax.dot_general(
        left, right, (((0,), (0,)), ((), ())), preferred_element_type=jnp.float32
    )


def place():
    return tuple(lax.axis_index(name) for name in ("z", "y", "c", "h", "s"))


def remote(source, target, sent, arrived, **device):
    return pltpu.make_async_remote_copy(
        src_ref=source,
        dst_ref=target,
        send_sem=sent,
        recv_sem=arrived,
        device_id=device,
        device_id_type=MESH,
    )


def greet(barrier, **device):
    pl.semaphore_signal(barrier, inc=1, device_id=device, device_id_type=MESH)


def rows_at(start, size):
    return pl.ds(pl.multiple_of(start, 16), size)


def shifted(z, y, step):
    at = z * NY + y + step
    return {"z": lax.div(at, NY), "y": lax.rem(at, NY)}


def has_neighbours(z, y):
    at = z * NY + y
    return at >= 2, at < NZ * NY - 2


def send_halo(z, y, ahead, behind, sent, arrived):
    before, after = has_neighbours(z, y)

    @pl.when(after)
    def _():
        remote(*ahead, sent.at[0], arrived.at[0], **shifted(z, y, 2)).start()

    @pl.when(before)
    def _():
        remote(*behind, sent.at[1], arrived.at[1], **shifted(z, y, -2)).start()


def wait_halo(z, y, ahead, behind, sent, arrived):
    before, after = has_neighbours(z, y)

    @pl.when(before)
    def _():
        remote(*ahead, sent.at[0], arrived.at[0], c=lax.axis_index("c")).wait_recv()

    @pl.when(jnp.logical_not(before))
    def _():
        ahead[1][...] = jnp.zeros_like(ahead[1])

    @pl.when(after)
    def _():
        remote(*behind, sent.at[1], arrived.at[1], c=lax.axis_index("c")).wait_recv()

    @pl.when(jnp.logical_not(after))
    def _():
        behind[1][...] = jnp.zeros_like(behind[1])


def drain_halo(z, y, ahead, behind, sent, arrived):
    before, after = has_neighbours(z, y)

    @pl.when(after)
    def _():
        remote(*ahead, sent.at[0], arrived.at[0], c=lax.axis_index("c")).wait_send()

    @pl.when(before)
    def _():
        remote(*behind, sent.at[1], arrived.at[1], c=lax.axis_index("c")).wait_send()


def greet_halo(barrier, z, y):
    before, after = has_neighbours(z, y)

    @pl.when(after)
    def _():
        greet(barrier, **shifted(z, y, 2))

    @pl.when(before)
    def _():
        greet(barrier, **shifted(z, y, -2))

    return before.astype(jnp.int32) + after.astype(jnp.int32)


COLS = 256
HALVES, PIECES = 2, 2


def cols_at(start, size):
    return pl.ds(pl.multiple_of(start, 128), size)


def repeat(count, step, start=0):
    def once(at, carry):
        step(at)
        return carry

    lax.fori_loop(start, count, once, 0)


YROWS, ZROWS, ZCUT = 40, 56, 32


def forward_kernel(
    feat, w3, tw, pw, mid_hbm, hid_hbm, block, act_hbm, twf,
    middle, hid_own, act_t, v_feat, v_w3, v_pw, own, act, ahead_out, behind_out, from_before, from_after, centre, hid_other, pwo,
    load, own_sem, halo_s, halo_r, hid_s, hid_r, x_s, x_r, y_s, y_r, pz_s, pz_r, tz_s, tz_r, sib_s, sib_r,
):
    z, y, c, h, s = place()
    bf16, f32 = jnp.bfloat16, jnp.float32
    channels = feat.shape[1]
    chunks = channels // COLS
    barrier = pltpu.get_barrier_semaphore()
    greet(barrier, h=1 - h)
    greet(barrier, s=1 - s)
    greet(barrier, c=1 - c)
    for step in (1, 2, NZ - 2, NZ - 1):
        greet(barrier, z=lax.rem(z + step, NZ))
    for step in range(1, NY):
        greet(barrier, y=lax.rem(y + step, NY))
    greeted = 10 + greet_halo(barrier, z, y)
    loads = [
        pltpu.make_async_copy(source, target, load.at[slot])
        for slot, (source, target) in enumerate(
            ((feat, v_feat), (w3.at[0], v_w3.at[0]), (w3.at[2], v_w3.at[2]), (w3.at[1], v_w3.at[1]), (pw, v_pw))
        )
    ]
    for copy in loads:
        copy.start()
    take_own = pltpu.make_async_copy(tw, own, own_sem.at[0])
    take_own.start()

    half = tw.shape[0] // 2
    point = pw.shape[0] // 2
    p_rows = point // 4
    other = 1 - s

    def rows8(start, size):
        return pl.ds(pl.multiple_of(start, 8), size)

    def y_rows(core, at):
        return rows8(core * half + at * YROWS, YROWS)

    def z_rows(core, at, cut):
        start = core * half + NY * YROWS + lax.rem(at, 4) * ZROWS
        return rows8(start, ZCUT) if cut == 0 else rows8(start + ZCUT, ZROWS - ZCUT)

    def p_rows_of(core, at, cut):
        start = core * point + lax.rem(at, 4) * p_rows
        if cut is None:
            return rows8(start, p_rows)
        return rows8(start + cut * (p_rows // 2), p_rows // 2)

    started = []

    def go(ref, target, sent, arrived, **device):
        copy = remote(ref, target, sent, arrived, **device)
        copy.start()
        started.append(copy)

    def landing(ref, sent, arrived):
        remote(ref, ref, sent, arrived, c=1 - c).wait_recv()

    pl.semaphore_wait(barrier, greeted)
    here = p_rows_of(c, z, None)
    go(pw.at[here], pwo.at[here], x_s.at[0], x_r.at[0], h=1 - h)
    for cut in range(2):
        here = z_rows(c, z, cut)
        go(tw.at[here], twf.at[s, here], x_s.at[1 + cut], x_r.at[1 + cut], s=1 - s)
    here = y_rows(c, y)
    go(tw.at[here], twf.at[s, here], x_s.at[3], x_r.at[3], s=1 - s)

    loads[0].wait()

    def act_step(at):
        cols = cols_at(at * COLS, COLS)
        act[:, cols] = gelu_value(v_feat[:, cols].astype(f32)).astype(bf16)

    repeat(chunks, act_step)
    before, after = has_neighbours(z, y)
    ahead, behind = (ahead_out, from_before), (behind_out, from_after)
    loads[1].wait()
    ahead_out[...] = times(act[...], v_w3[0]).astype(bf16)

    @pl.when(after)
    def _():
        remote(*ahead, halo_s.at[0], halo_r.at[0], **shifted(z, y, 2)).start()

    loads[2].wait()
    behind_out[...] = times(act[...], v_w3[2]).astype(bf16)

    @pl.when(before)
    def _():
        remote(*behind, halo_s.at[1], halo_r.at[1], **shifted(z, y, -2)).start()

    steps = (1, NZ - 1, 2, NZ - 2)
    here = pwo.at[p_rows_of(c, z, None)]
    landing(here, x_s.at[0], x_r.at[0])
    for slot in range(2):
        go(here, here, pz_s.at[slot], pz_r.at[slot], z=lax.rem(z + steps[slot], NZ))
    for cut in range(2):
        piece = pwo.at[p_rows_of(c, z, cut)]
        go(piece, piece, pz_s.at[2 + cut], pz_r.at[2 + cut], z=lax.rem(z + steps[2 + cut], NZ))
    go(here, here, sib_s.at[0], sib_r.at[0], c=1 - c)
    for cut in range(2):
        here = twf.at[other, z_rows(c, z, cut)]
        landing(here, x_s.at[1 + cut], x_r.at[1 + cut])
        for slot, step in enumerate((steps[0], steps[1], steps[2 + cut])):
            go(here, here, tz_s.at[cut, slot], tz_r.at[cut, slot], z=lax.rem(z + step, NZ))
        go(here, here, sib_s.at[5 + cut], sib_r.at[5 + cut], c=1 - c)
        if cut == 0:
            loads[3].wait()
            centre[...] = times(act[...], v_w3[1])
    here = twf.at[other, y_rows(c, y)]
    landing(here, x_s.at[3], x_r.at[3])
    for step in range(1, NY):
        go(here, here, y_s.at[step - 1], y_r.at[step - 1], y=lax.rem(y + step, NY))
    go(here, here, sib_s.at[13], sib_r.at[13], c=1 - c)
    take_own.wait()
    put_own = pltpu.make_async_copy(own, twf.at[s], own_sem.at[1])
    put_own.start()

    def turn_step(at):
        act_t[rows_at(at * COLS, COLS), :] = act[:, cols_at(at * COLS, COLS)].T

    repeat(chunks, turn_step)
    stores = [
        pltpu.make_async_copy(source, target, load.at[5 + slot])
        for slot, (source, target) in enumerate(((act_t, act_hbm), (middle, mid_hbm), (hid_own, hid_hbm)))
    ]
    stores[0].start()

    def p_from(core, slot):
        at = z + NZ - steps[slot]
        return pwo.at[p_rows_of(core, at, None if slot < 2 else slot - 2)]

    def t_from(core, cut, slot):
        step = steps[slot] if slot < 2 else steps[2 + cut]
        return twf.at[other, z_rows(core, z + NZ - step, cut)]

    def y_from(core, step):
        return twf.at[other, y_rows(core, lax.rem(y + NY - step, NY))]

    for slot in range(4):
        here = p_from(c, slot)
        landing(here, pz_s.at[slot], pz_r.at[slot])
        go(here, here, sib_s.at[1 + slot], sib_r.at[1 + slot], c=1 - c)

    wait_halo(z, y, ahead, behind, halo_s, halo_r)
    total = centre[...] + from_before[...].astype(f32) + from_after[...].astype(f32)
    middle[...] = total
    hid_own[...] = gelu_value(total).astype(bf16)
    go(hid_own, hid_other, hid_s, hid_r, h=1 - h)
    stores[1].start()
    stores[2].start()

    def take_z(cut):
        for slot in range(3):
            here = t_from(c, cut, slot)
            landing(here, tz_s.at[cut, slot], tz_r.at[cut, slot])
            at = 7 + cut * 3 + slot
            go(here, here, sib_s.at[at], sib_r.at[at], c=1 - c)

    take_z(0)
    landing(pwo.at[p_rows_of(1 - c, z, None)], sib_s.at[0], sib_r.at[0])
    for slot in range(4):
        landing(p_from(1 - c, slot), sib_s.at[1 + slot], sib_r.at[1 + slot])
    loads[4].wait()
    landing(hid_other, hid_s, hid_r)

    def block_step(at):
        cols, where = cols_at(at * COLS, COLS), rows_at(at * COLS, COLS)
        value = v_feat[:, cols].astype(f32)
        value = value + times_transposed(hid_own[...], v_pw[where, :])
        value = value + times_transposed(hid_other[...], pwo[where, :])
        block[:, cols] = value.astype(bf16)

    repeat(chunks, block_step)
    take_z(1)
    for step in range(1, NY):
        here = y_from(c, step)
        landing(here, y_s.at[step - 1], y_r.at[step - 1])
        go(here, here, sib_s.at[13 + step], sib_r.at[13 + step], c=1 - c)

    for cut in range(2):
        landing(twf.at[other, z_rows(1 - c, z, cut)], sib_s.at[5 + cut], sib_r.at[5 + cut])
        for slot in range(3):
            at = 7 + cut * 3 + slot
            landing(t_from(1 - c, cut, slot), sib_s.at[at], sib_r.at[at])
    landing(twf.at[other, y_rows(1 - c, y)], sib_s.at[13], sib_r.at[13])
    for step in range(1, NY):
        landing(y_from(1 - c, step), sib_s.at[13 + step], sib_r.at[13 + step])
    for copy in started:
        copy.wait_send()
    drain_halo(z, y, ahead, behind, halo_s, halo_r)
    put_own.wait()
    for copy in stores:
        copy.wait()


def forward_exchange(feat, w3, tw, pw):
    bf16, f32 = jnp.bfloat16, jnp.float32
    positions, channels = feat.shape
    width = pw.shape[1]
    return pl.pallas_call(
        forward_kernel,
        out_shape=(
            jax.ShapeDtypeStruct((positions, width), f32),
            jax.ShapeDtypeStruct((positions, width), bf16),
            jax.ShapeDtypeStruct((positions, channels), bf16),
            jax.ShapeDtypeStruct((channels, positions), bf16),
            jax.ShapeDtypeStruct((2, *tw.shape), bf16),
        ),
        in_specs=[ANY, ANY, ANY, ANY],
        out_specs=(ANY, ANY, VMEM, ANY, ANY),
        scratch_shapes=[
            pltpu.VMEM((positions, width), f32),
            pltpu.VMEM((positions, width), bf16),
            pltpu.VMEM((channels, positions), bf16),
            pltpu.VMEM(feat.shape, bf16),
            pltpu.VMEM(w3.shape, bf16),
            pltpu.VMEM(pw.shape, bf16),
            pltpu.VMEM(tw.shape, bf16),
            pltpu.VMEM(feat.shape, bf16),
            pltpu.VMEM((positions, width), bf16),
            pltpu.VMEM((positions, width), bf16),
            pltpu.VMEM((positions, width), bf16),
            pltpu.VMEM((positions, width), bf16),
            pltpu.VMEM((positions, width), f32),
            pltpu.VMEM((positions, width), bf16),
            pltpu.VMEM(pw.shape, bf16),
            DMA((8,)), DMA((2,)),
            DMA((2,)), DMA((2,)),
            DMA, DMA,
            DMA((4,)), DMA((4,)),
            DMA((3,)), DMA((3,)),
            DMA((4,)), DMA((4,)),
            DMA((2, 3)), DMA((2, 3)),
            DMA((17,)), DMA((17,)),
        ],
        compiler_params=pltpu.CompilerParams(
            collective_id=0, has_side_effects=True, vmem_limit_bytes=67043328
        ),
        name="forward_exchange",
    )(feat, w3, tw, pw)


def backward_kernel(
    feat, hid_hbm, mid_hbm, block_hbm, act_hbm, tw, cot, pw, w3, grad_out, summed,
    hidden, middle, v_feat, block, act_t, v_tw, v_cot, v_pw, v_w3, score, out_grad, slope_f, slope_m,
    hid_grad, mid_grad, later, earlier, swap_out, swap_in, act_out, act_in,
    early, late, sib_early, sib_late, ring_out, ring_in, final, early_out, early_in,
    y_out, y_in, z_tile, z_out, z_in,
    load, tw_load, swap_s, swap_r, acts_s, acts_r, halo_s, halo_r, sibe_s, sibe_r, sibl_s, sibl_r,
    ring_s, ring_r, fin_s, fin_r, y_s, y_r, z_s, z_r,
):
    z, y, c, h, s = place()
    up, down = lax.rem(z + 1, NZ), lax.rem(z + NZ - 1, NZ)
    me = (y * 2 + c) * 2 + s
    corner = c * 2 + s
    channels, tracks = tw.shape
    chunks = channels // COLS
    rows = channels // NZ
    part = rows // NY
    each = part // 4
    sub = rows // HALVES // PIECES
    bf16, f32 = jnp.bfloat16, jnp.float32

    def group(at):
        return {"y": lax.div(at, 4), "c": lax.rem(lax.div(at, 2), 2), "s": lax.rem(at, 2)}

    def corner_of(at):
        return {"c": lax.div(at, 2), "s": lax.rem(at, 2)}

    barrier = pltpu.get_barrier_semaphore()
    greet(barrier, h=1 - h)
    for step in range(1, 16):
        greet(barrier, **group(lax.rem(me + step, 16)))
    for step in range(1, NZ):
        for turn in range(4):
            greet(barrier, z=lax.rem(z + step, NZ), **corner_of(turn))
    greeted = 1 + 15 + 4 * (NZ - 1) + greet_halo(barrier, z, y)

    loads = [
        pltpu.make_async_copy(source, target, load.at[slot])
        for slot, (source, target) in enumerate(
            ((block_hbm, block), (cot, v_cot), (feat, v_feat), (pw, v_pw), (act_hbm, act_t), (w3, v_w3), (hid_hbm, hidden), (mid_hbm, middle))
        )
    ]
    whole, tail = tracks // COLS, tracks % COLS

    def tw_copy(at, size=COLS):
        where = cols_at(at * COLS, size)
        return pltpu.make_async_copy(tw.at[:, where], v_tw.at[:, where], tw_load.at[at])

    loads[0].start()
    loads[1].start()
    repeat(whole, lambda at: tw_copy(at).start())
    tw_copy(whole, tail).start()
    loads[0].wait()
    loads[1].wait()

    def score_step(at, size=COLS):
        tw_copy(at, size).wait()
        cols = cols_at(at * COLS, size)
        value = jax.nn.sigmoid(times(block[...], v_tw[:, cols]))
        score[:, cols] = (v_cot[:, cols].astype(f32) * value).astype(bf16)

    repeat(whole, score_step)
    score_step(whole, tail)
    for copy in loads[2:]:
        copy.start()
    pl.semaphore_wait(barrier, greeted)

    def swap_copy(at):
        return remote(swap_out.at[at], swap_in.at[at], swap_s.at[at], swap_r.at[at], h=1 - h)

    def swap_step(at):
        swap_out[at] = times_transposed(score[...], v_tw[rows_at(at * COLS, COLS), :]).astype(bf16)
        swap_copy(at).start()

    repeat(chunks, swap_step)
    for slot in (2, 3, 6, 7):
        loads[slot].wait()
    slope_m[...] = gelu_slope(middle[...])
    hid_grad[...] = jnp.zeros_like(hid_grad)

    def slope_step(at):
        cols = cols_at(at * COLS, COLS)
        slope_f[at] = gelu_slope(v_feat[:, cols].astype(f32))

    repeat(chunks, slope_step)

    def gather_step(at):
        swap_copy(at).wait_recv()
        where = rows_at(at * COLS, COLS)
        value = swap_out[at].astype(f32) + swap_in[at].astype(f32)
        out_grad[at] = value
        rounded = value.astype(bf16)
        hid_grad[...] += times(rounded, v_pw[where, :])
        early[0, where, :] = transposed_times(rounded, hidden[...]).astype(bf16)

    repeat(chunks, gather_step)
    mid_grad[...] = (hid_grad[...] * slope_m[...]).astype(bf16)
    ahead, behind = (mid_grad, earlier), (mid_grad, later)
    send_halo(z, y, ahead, behind, halo_s, halo_r)

    loads[4].wait()

    def centre_step(at):
        where = rows_at(at * rows, rows)
        early[1, where, :] = times(act_t[where, :], mid_grad[...]).astype(bf16)

    repeat(NZ, centre_step)
    order = (7, 1, 6, 2, 5, 3, 4, 0)

    def early_sibling(slot):
        where = rows_at(lax.rem(z + order[slot], NZ) * rows, rows)
        return remote(early.at[1 - c, where], sib_early.at[where], sibe_s.at[slot], sibe_r.at[slot], c=1 - c)

    for slot in range(NZ):
        early_sibling(slot).start()

    def partial(at, way, piece):
        where = rows_at(at * rows + (way * PIECES + piece) * sub, sub)
        return early[c, where, :].astype(f32) + sib_early[where, :].astype(f32)

    def ring_copy(step, way, piece):
        return remote(
            ring_out.at[step, way, piece], ring_in.at[step, way, piece],
            ring_s.at[step, way, piece], ring_r.at[step, way, piece], z=up if way == 0 else down,
        )

    def ring_step(step):
        for piece in range(PIECES):
            for way in range(HALVES):
                at = lax.rem(z + NZ - 1 - step, NZ) if way == 0 else lax.rem(z + 1 + step, NZ)
                value = partial(at, way, piece)
                if step:
                    ring_copy(step - 1, way, piece).wait_recv()
                    value = value + ring_in[step - 1, way, piece].astype(f32)
                ring_out[step, way, piece] = value.astype(bf16)
                ring_copy(step, way, piece).start()

    early_sibling(0).wait_recv()
    early_sibling(1).wait_recv()
    ring_step(0)
    for slot in range(2, NZ):
        early_sibling(slot).wait_recv()
    ring_step(1)
    ring_step(2)
    wait_halo(z, y, ahead, behind, halo_s, halo_r)

    def late_sibling(at):
        where = rows_at(at * rows, rows)
        return remote(late.at[1 - c, where], sib_late.at[where], sibl_s.at[at], sibl_r.at[at], c=1 - c)

    def late_step(turn):
        at = lax.rem(z + turn, NZ)
        where = rows_at(at * rows, rows)
        late[0, where, :] = times(act_t[where, :], later[...]).astype(bf16)
        late[1, where, :] = times(act_t[where, :], earlier[...]).astype(bf16)
        late_sibling(at).start()

    def y_copy(at, step):
        return remote(
            y_out.at[at, rows_at(lax.rem(y + step, NY) * part, part)], y_in.at[at, step - 1],
            y_s.at[at, step - 1], y_r.at[at, step - 1], y=lax.rem(y + step, NY),
        )

    def y_step(turn):
        at = lax.rem(z + turn, NZ)
        where = rows_at(at * rows, rows)
        late_sibling(at).wait_recv()
        y_out[at] = (late[c, where, :].astype(f32) + sib_late[where, :].astype(f32)).astype(bf16)
        for step in range(1, NY):
            y_copy(at, step).start()

    def act_copy(at):
        return remote(act_out.at[at], act_in.at[at], acts_s.at[at], acts_r.at[at], h=1 - h)

    def act_step(at):
        where = rows_at(at * COLS, COLS)
        value = times_transposed(later[...], v_w3[0, where, :])
        value = value + times_transposed(mid_grad[...], v_w3[1, where, :])
        value = value + times_transposed(earlier[...], v_w3[2, where, :])
        act_out[at] = value.astype(bf16)
        act_copy(at).start()

    def mixed_step(turn):
        act_step(turn - 1)
        late_step(turn + 1)
        y_step(turn)

    loads[5].wait()
    late_step(1)
    repeat(chunks // 2 + 1, mixed_step, 1)
    ring_step(3)
    repeat(chunks + 1, mixed_step, chunks // 2 + 1)
    ring_step(4)
    late_step(NZ)
    y_step(NZ - 1)
    y_step(NZ)

    def z_copy(turn, at, twist):
        to = lax.rem(corner + twist, 4)
        return remote(
            z_out.at[at, to], z_in.at[z, corner], z_s.at[turn - 1, twist], z_r.at[turn - 1, twist],
            z=at, **corner_of(to),
        )

    def z_sum(turn):
        at = lax.rem(z + turn, NZ)
        where = rows_at(at * rows + y * part, part)
        value = late[c, where, :].astype(f32) + sib_late[where, :].astype(f32)
        for step in range(1, NY):
            y_copy(at, step).wait_recv()
            value = value + y_in[at, step - 1].astype(f32)
        z_tile[...] = value
        for to in range(4):
            z_out[at, to] = z_tile[to * each:(to + 1) * each, :].astype(bf16)
        return at

    def z_step(turn):
        at = z_sum(turn)
        for twist in range(4):
            z_copy(turn, at, twist).start()

    z_step(1)
    z_step(2)
    ring_step(5)
    z_step(3)
    z_step(4)
    ring_step(6)
    z_step(5)
    z_step(6)
    z_step(7)
    z_sum(NZ)
    for twist in range(1, 4):
        z_copy(NZ, z, twist).start()
    z_in[z, corner] = z_out[z, corner]

    for piece in range(PIECES):
        for way in range(HALVES):
            value = partial(z, way, piece)
            ring_copy(NZ - 2, way, piece).wait_recv()
            value = value + ring_in[NZ - 2, way, piece].astype(f32)
            final[(way * PIECES + piece) * sub:(way * PIECES + piece + 1) * sub, :] = value
    for at in range(16):
        early_out[at] = final[at * each:(at + 1) * each, :].astype(bf16)

    def fin_copy(step):
        to = lax.rem(me + step, 16)
        return remote(early_out.at[to], early_in.at[me], fin_s.at[step - 1], fin_r.at[step - 1], **group(to))

    for step in range(1, 16):
        fin_copy(step).start()
    early_in[me] = early_out[me]

    def out_step(at):
        act_copy(at).wait_recv()
        value = act_out[at].astype(f32) + act_in[at].astype(f32)
        grad_out[:, cols_at(at * COLS, COLS)] = (out_grad[at] + value * slope_f[at]).astype(bf16)

    repeat(chunks, out_step)
    for turn in range(1, NZ + 1):
        for twist in range(1 if turn == NZ else 0, 4):
            source = lax.rem(z + 2 * NZ - turn, NZ)
            ref = z_in.at[source, lax.rem(corner + 4 - twist, 4)]
            remote(ref, ref, z_s.at[turn - 1, twist], z_r.at[turn - 1, twist], z=z).wait_recv()
    for core in range(2):
        total = jnp.zeros((each, hidden.shape[1]), f32)
        for turn in range(NZ):
            for sample in range(2):
                total = total + z_in[turn, core * 2 + sample].astype(f32)
        summed[2 + core] = total
    for step in range(1, 16):
        ref = early_in.at[lax.rem(me + 16 - step, 16)]
        remote(ref, ref, fin_s.at[step - 1], fin_r.at[step - 1], z=z).wait_recv()
    for core in range(2):
        total = jnp.zeros((each, hidden.shape[1]), f32)
        for row in range(NY):
            for sample in range(2):
                total = total + early_in[(row * 2 + core) * 2 + sample].astype(f32)
        summed[core] = total

    def drain_chunks(at):
        swap_copy(at).wait_send()
        act_copy(at).wait_send()

    repeat(chunks, drain_chunks)
    drain_halo(z, y, ahead, behind, halo_s, halo_r)
    for slot in range(NZ):
        early_sibling(slot).wait_send()
    for step in range(NZ - 1):
        for piece in range(PIECES):
            for way in range(HALVES):
                ring_copy(step, way, piece).wait_send()

    def drain_late(at):
        late_sibling(at).wait_send()
        for step in range(1, NY):
            y_copy(at, step).wait_send()

    repeat(NZ, drain_late)
    for turn in range(1, NZ + 1):
        for twist in range(1 if turn == NZ else 0, 4):
            z_copy(turn, lax.rem(z + turn, NZ), twist).wait_send()
    for step in range(1, 16):
        fin_copy(step).wait_send()


def backward(feat, hidden, middle, block, act_t, tw, cot, pw, w3):
    bf16, f32 = jnp.bfloat16, jnp.float32
    positions, channels = feat.shape
    width = pw.shape[1]
    tracks = tw.shape[1]
    chunks = channels // COLS
    rows = channels // NZ
    part = rows // NY
    each = part // 4
    sub = rows // HALVES // PIECES
    ring = (NZ - 1, HALVES, PIECES)
    tile = (chunks, positions, COLS)
    return pl.pallas_call(
        backward_kernel,
        out_shape=(
            jax.ShapeDtypeStruct((positions, channels), bf16),
            jax.ShapeDtypeStruct((4, each, width), f32),
        ),
        in_specs=[ANY] * 9,
        out_specs=(VMEM, VMEM),
        scratch_shapes=[
            pltpu.VMEM(hidden.shape, bf16),
            pltpu.VMEM(middle.shape, f32),
            pltpu.VMEM(feat.shape, bf16),
            pltpu.VMEM(feat.shape, bf16),
            pltpu.VMEM(act_t.shape, bf16),
            pltpu.VMEM(tw.shape, bf16),
            pltpu.VMEM(cot.shape, bf16),
            pltpu.VMEM(pw.shape, bf16),
            pltpu.VMEM(w3.shape, bf16),
            pltpu.VMEM((positions, tracks), bf16),
            pltpu.VMEM(tile, f32),
            pltpu.VMEM(tile, f32),
            pltpu.VMEM((positions, width), f32),
            pltpu.VMEM((positions, width), f32),
            pltpu.VMEM((positions, width), bf16),
            pltpu.VMEM((positions, width), bf16),
            pltpu.VMEM((positions, width), bf16),
            pltpu.VMEM(tile, bf16),
            pltpu.VMEM(tile, bf16),
            pltpu.VMEM(tile, bf16),
            pltpu.VMEM(tile, bf16),
            pltpu.VMEM((2, channels, width), bf16),
            pltpu.VMEM((2, channels, width), bf16),
            pltpu.VMEM((channels, width), bf16),
            pltpu.VMEM((channels, width), bf16),
            pltpu.VMEM((*ring, sub, width), bf16),
            pltpu.VMEM((*ring, sub, width), bf16),
            pltpu.VMEM((rows, width), f32),
            pltpu.VMEM((16, each, width), bf16),
            pltpu.VMEM((16, each, width), bf16),
            pltpu.VMEM((NZ, rows, width), bf16),
            pltpu.VMEM((NZ, NY - 1, part, width), bf16),
            pltpu.VMEM((part, width), f32),
            pltpu.VMEM((NZ, 4, each, width), bf16),
            pltpu.VMEM((NZ, 4, each, width), bf16),
            DMA((8,)), DMA((tracks // COLS + 1,)),
            DMA((chunks,)), DMA((chunks,)),
            DMA((chunks,)), DMA((chunks,)),
            DMA((2,)), DMA((2,)),
            DMA((NZ,)), DMA((NZ,)),
            DMA((NZ,)), DMA((NZ,)),
            DMA(ring), DMA(ring),
            DMA((15,)), DMA((15,)),
            DMA((NZ, NY - 1)), DMA((NZ, NY - 1)),
            DMA((NZ, 4)), DMA((NZ, 4)),
        ],
        compiler_params=pltpu.CompilerParams(
            collective_id=1, has_side_effects=True, vmem_limit_bytes=60000000
        ),
        name="backward",
    )(feat, hidden, middle, block, act_t, tw, cot, pw, w3)


def body(features, dilated_weight, point_weight, track_weight, track_cotangent):
    samples, positions, channels = features.shape
    number_rows = samples * positions
    feat = features.reshape(number_rows, channels)
    taps_weight = jnp.transpose(dilated_weight, (1, 0, 2))
    middle, hidden, block, turned, whole_track = forward_exchange(
        feat, taps_weight, track_weight, point_weight
    )
    whole_track = whole_track.reshape(channels, track_weight.shape[1])
    cotangent = track_cotangent.reshape(number_rows, whole_track.shape[1])
    input_grad, summed = backward(
        feat, hidden, middle, block, turned, whole_track, cotangent, point_weight, taps_weight
    )
    dilated_grad = jnp.stack([summed[2], summed[1], summed[3]], axis=1)
    return (input_grad.reshape(samples, positions, channels), dilated_grad, summed[0])


def solution(mesh):
    torus = Mesh(
        mesh.devices.reshape(NZ, NY, 2, mesh.shape["head"], mesh.shape["sample"]),
        ("z", "y", "c", "h", "s"),
    )
    placed = (
        P("s", SEQ, None),
        P(None, None, "h"),
        P(None, "h"),
        P("s", "h"),
        P("s", SEQ, "h"),
    )
    return jax.shard_map(
        body,
        mesh=torus,
        in_specs=placed,
        out_specs=(P("s", SEQ, None), P(SEQ_SAMPLE, None, "h"), P(SEQ_SAMPLE, "h")),
        check_vma=False,
    )
```

```python
import jax
import jax.numpy as jnp
from jax import lax
from jax.experimental import pallas as pl
from jax.experimental.pallas import tpu as pltpu
from jax.sharding import Mesh
from jax.sharding import PartitionSpec as P

MESH = pl.DeviceIdType.MESH
SEQ = ("z", "y", "c")
SEQ_SAMPLE = ("z", "y", "c", "s")
NZ, NY = 8, 4
VMEM = pl.BlockSpec(memory_space=pltpu.VMEM)
ANY = pl.BlockSpec(memory_space=pltpu.HBM)
DMA = pltpu.SemaphoreType.DMA


def gelu_value(value):
    inner = 0.7978845608 * (value + 0.044715 * value * value * value)
    return 0.5 * value * (1.0 + jnp.tanh(inner))


def gelu_slope(value):
    inner = 0.7978845608 * (value + 0.044715 * value * value * value)
    tangent = jnp.tanh(inner)
    return 0.5 * (1.0 + tangent) + 0.5 * value * (1.0 - tangent * tangent) * 0.7978845608 * (
        1.0 + 3.0 * 0.044715 * value * value
    )


def times(left, right):
    return jnp.dot(left, right, preferred_element_type=jnp.float32)


def times_transposed(left, right):
    return lax.dot_general(
        left, right, (((1,), (1,)), ((), ())), preferred_element_type=jnp.float32
    )


def transposed_times(left, right):
    return lax.dot_general(
        left, right, (((0,), (0,)), ((), ())), preferred_element_type=jnp.float32
    )


def place():
    return tuple(lax.axis_index(name) for name in ("z", "y", "c", "h", "s"))


def remote(source, target, sent, arrived, **device):
    return pltpu.make_async_remote_copy(
        src_ref=source,
        dst_ref=target,
        send_sem=sent,
        recv_sem=arrived,
        device_id=device,
        device_id_type=MESH,
    )


def greet(barrier, **device):
    pl.semaphore_signal(barrier, inc=1, device_id=device, device_id_type=MESH)


def rows_at(start, size):
    return pl.ds(pl.multiple_of(start, 16), size)


def shifted(z, y, step):
    at = z * NY + y + step
    return {"z": lax.div(at, NY), "y": lax.rem(at, NY)}


def has_neighbours(z, y):
    at = z * NY + y
    return at >= 2, at < NZ * NY - 2


def send_halo(z, y, ahead, behind, sent, arrived):
    before, after = has_neighbours(z, y)

    @pl.when(after)
    def _():
        remote(*ahead, sent.at[0], arrived.at[0], **shifted(z, y, 2)).start()

    @pl.when(before)
    def _():
        remote(*behind, sent.at[1], arrived.at[1], **shifted(z, y, -2)).start()


def wait_halo(z, y, ahead, behind, sent, arrived):
    before, after = has_neighbours(z, y)

    @pl.when(before)
    def _():
        remote(*ahead, sent.at[0], arrived.at[0], c=lax.axis_index("c")).wait_recv()

    @pl.when(jnp.logical_not(before))
    def _():
        ahead[1][...] = jnp.zeros_like(ahead[1])

    @pl.when(after)
    def _():
        remote(*behind, sent.at[1], arrived.at[1], c=lax.axis_index("c")).wait_recv()

    @pl.when(jnp.logical_not(after))
    def _():
        behind[1][...] = jnp.zeros_like(behind[1])


def drain_halo(z, y, ahead, behind, sent, arrived):
    before, after = has_neighbours(z, y)

    @pl.when(after)
    def _():
        remote(*ahead, sent.at[0], arrived.at[0], c=lax.axis_index("c")).wait_send()

    @pl.when(before)
    def _():
        remote(*behind, sent.at[1], arrived.at[1], c=lax.axis_index("c")).wait_send()


def greet_halo(barrier, z, y):
    before, after = has_neighbours(z, y)

    @pl.when(after)
    def _():
        greet(barrier, **shifted(z, y, 2))

    @pl.when(before)
    def _():
        greet(barrier, **shifted(z, y, -2))

    return before.astype(jnp.int32) + after.astype(jnp.int32)


COLS = 256
HALVES, PIECES = 2, 2


def cols_at(start, size):
    return pl.ds(pl.multiple_of(start, 128), size)


def repeat(count, step, start=0):
    def once(at, carry):
        step(at)
        return carry

    lax.fori_loop(start, count, once, 0)


YROWS, ZROWS, ZCUT = 40, 56, 32


def forward_kernel(
    feat, w3, tw, pw, mid_hbm, hid_hbm, block, act_hbm, twf,
    middle, hid_own, act_t, v_feat, v_w3, v_pw, own, act, ahead_out, behind_out, from_before, from_after, centre, hid_other, pwo,
    load, own_sem, halo_s, halo_r, hid_s, hid_r, x_s, x_r, y_s, y_r, pz_s, pz_r, tz_s, tz_r, sib_s, sib_r,
):
    z, y, c, h, s = place()
    bf16, f32 = jnp.bfloat16, jnp.float32
    channels = feat.shape[1]
    chunks = channels // COLS
    barrier = pltpu.get_barrier_semaphore()
    greet(barrier, h=1 - h)
    greet(barrier, s=1 - s)
    greet(barrier, c=1 - c)
    for step in (1, 2, NZ - 2, NZ - 1):
        greet(barrier, z=lax.rem(z + step, NZ))
    for step in range(1, NY):
        greet(barrier, y=lax.rem(y + step, NY))
    greeted = 10 + greet_halo(barrier, z, y)
    loads = [
        pltpu.make_async_copy(source, target, load.at[slot])
        for slot, (source, target) in enumerate(
            ((feat, v_feat), (w3.at[0], v_w3.at[0]), (w3.at[2], v_w3.at[2]), (w3.at[1], v_w3.at[1]), (pw, v_pw))
        )
    ]
    for copy in loads[:3]:
        copy.start()

    half = tw.shape[0] // 2
    point = pw.shape[0] // 2
    p_rows = point // 4
    other = 1 - s

    def rows8(start, size):
        return pl.ds(pl.multiple_of(start, 8), size)

    def y_rows(core, at):
        return rows8(core * half + at * YROWS, YROWS)

    def z_rows(core, at, cut):
        start = core * half + NY * YROWS + lax.rem(at, 4) * ZROWS
        return rows8(start, ZCUT) if cut == 0 else rows8(start + ZCUT, ZROWS - ZCUT)

    def p_rows_of(core, at, cut):
        start = core * point + lax.rem(at, 4) * p_rows
        if cut is None:
            return rows8(start, p_rows)
        return rows8(start + cut * (p_rows // 2), p_rows // 2)

    started = []

    def go(ref, target, sent, arrived, **device):
        copy = remote(ref, target, sent, arrived, **device)
        copy.start()
        started.append(copy)

    def landing(ref, sent, arrived):
        remote(ref, ref, sent, arrived, c=1 - c).wait_recv()

    pl.semaphore_wait(barrier, greeted)
    here = p_rows_of(c, z, None)
    go(pw.at[here], pwo.at[here], x_s.at[0], x_r.at[0], h=1 - h)
    for cut in range(2):
        here = z_rows(c, z, cut)
        go(tw.at[here], twf.at[s, here], x_s.at[1 + cut], x_r.at[1 + cut], s=1 - s)
    here = y_rows(c, y)
    go(tw.at[here], twf.at[s, here], x_s.at[3], x_r.at[3], s=1 - s)

    loads[0].wait()

    def act_step(at):
        cols = cols_at(at * COLS, COLS)
        act[:, cols] = gelu_value(v_feat[:, cols].astype(f32)).astype(bf16)

    repeat(chunks, act_step)
    before, after = has_neighbours(z, y)
    ahead, behind = (ahead_out, from_before), (behind_out, from_after)
    loads[1].wait()
    ahead_out[...] = times(act[...], v_w3[0]).astype(bf16)

    @pl.when(after)
    def _():
        remote(*ahead, halo_s.at[0], halo_r.at[0], **shifted(z, y, 2)).start()

    loads[2].wait()
    behind_out[...] = times(act[...], v_w3[2]).astype(bf16)

    @pl.when(before)
    def _():
        remote(*behind, halo_s.at[1], halo_r.at[1], **shifted(z, y, -2)).start()

    for copy in loads[3:]:
        copy.start()
    take_own = pltpu.make_async_copy(tw, own, own_sem.at[0])
    take_own.start()
    steps = (1, NZ - 1, 2, NZ - 2)
    here = pwo.at[p_rows_of(c, z, None)]
    landing(here, x_s.at[0], x_r.at[0])
    for slot in range(2):
        go(here, here, pz_s.at[slot], pz_r.at[slot], z=lax.rem(z + steps[slot], NZ))
    for cut in range(2):
        piece = pwo.at[p_rows_of(c, z, cut)]
        go(piece, piece, pz_s.at[2 + cut], pz_r.at[2 + cut], z=lax.rem(z + steps[2 + cut], NZ))
    go(here, here, sib_s.at[0], sib_r.at[0], c=1 - c)
    for cut in range(2):
        here = twf.at[other, z_rows(c, z, cut)]
        landing(here, x_s.at[1 + cut], x_r.at[1 + cut])
        for slot, step in enumerate((steps[0], steps[1], steps[2 + cut])):
            go(here, here, tz_s.at[cut, slot], tz_r.at[cut, slot], z=lax.rem(z + step, NZ))
        go(here, here, sib_s.at[5 + cut], sib_r.at[5 + cut], c=1 - c)
        if cut == 0:
            loads[3].wait()
            centre[...] = times(act[...], v_w3[1])
    here = twf.at[other, y_rows(c, y)]
    landing(here, x_s.at[3], x_r.at[3])
    for step in range(1, NY):
        go(here, here, y_s.at[step - 1], y_r.at[step - 1], y=lax.rem(y + step, NY))
    go(here, here, sib_s.at[13], sib_r.at[13], c=1 - c)
    take_own.wait()
    put_own = pltpu.make_async_copy(own, twf.at[s], own_sem.at[1])
    put_own.start()

    def turn_step(at):
        act_t[rows_at(at * COLS, COLS), :] = act[:, cols_at(at * COLS, COLS)].T

    repeat(chunks, turn_step)
    stores = [
        pltpu.make_async_copy(source, target, load.at[5 + slot])
        for slot, (source, target) in enumerate(((act_t, act_hbm), (middle, mid_hbm), (hid_own, hid_hbm)))
    ]
    stores[0].start()

    def p_from(core, slot):
        at = z + NZ - steps[slot]
        return pwo.at[p_rows_of(core, at, None if slot < 2 else slot - 2)]

    def t_from(core, cut, slot):
        step = steps[slot] if slot < 2 else steps[2 + cut]
        return twf.at[other, z_rows(core, z + NZ - step, cut)]

    def y_from(core, step):
        return twf.at[other, y_rows(core, lax.rem(y + NY - step, NY))]

    for slot in range(4):
        here = p_from(c, slot)
        landing(here, pz_s.at[slot], pz_r.at[slot])
        go(here, here, sib_s.at[1 + slot], sib_r.at[1 + slot], c=1 - c)

    wait_halo(z, y, ahead, behind, halo_s, halo_r)
    total = centre[...] + from_before[...].astype(f32) + from_after[...].astype(f32)
    middle[...] = total
    hid_own[...] = gelu_value(total).astype(bf16)
    go(hid_own, hid_other, hid_s, hid_r, h=1 - h)
    stores[1].start()
    stores[2].start()

    def take_z(cut):
        for slot in range(3):
            here = t_from(c, cut, slot)
            landing(here, tz_s.at[cut, slot], tz_r.at[cut, slot])
            at = 7 + cut * 3 + slot
            go(here, here, sib_s.at[at], sib_r.at[at], c=1 - c)

    take_z(0)
    landing(pwo.at[p_rows_of(1 - c, z, None)], sib_s.at[0], sib_r.at[0])
    for slot in range(4):
        landing(p_from(1 - c, slot), sib_s.at[1 + slot], sib_r.at[1 + slot])
    loads[4].wait()
    landing(hid_other, hid_s, hid_r)

    def block_step(at):
        cols, where = cols_at(at * COLS, COLS), rows_at(at * COLS, COLS)
        value = v_feat[:, cols].astype(f32)
        value = value + times_transposed(hid_own[...], v_pw[where, :])
        value = value + times_transposed(hid_other[...], pwo[where, :])
        block[:, cols] = value.astype(bf16)

    repeat(chunks, block_step)
    take_z(1)
    for step in range(1, NY):
        here = y_from(c, step)
        landing(here, y_s.at[step - 1], y_r.at[step - 1])
        go(here, here, sib_s.at[13 + step], sib_r.at[13 + step], c=1 - c)

    for cut in range(2):
        landing(twf.at[other, z_rows(1 - c, z, cut)], sib_s.at[5 + cut], sib_r.at[5 + cut])
        for slot in range(3):
            at = 7 + cut * 3 + slot
            landing(t_from(1 - c, cut, slot), sib_s.at[at], sib_r.at[at])
    landing(twf.at[other, y_rows(1 - c, y)], sib_s.at[13], sib_r.at[13])
    for step in range(1, NY):
        landing(y_from(1 - c, step), sib_s.at[13 + step], sib_r.at[13 + step])
    for copy in started:
        copy.wait_send()
    drain_halo(z, y, ahead, behind, halo_s, halo_r)
    put_own.wait()
    for copy in stores:
        copy.wait()


def forward_exchange(feat, w3, tw, pw):
    bf16, f32 = jnp.bfloat16, jnp.float32
    positions, channels = feat.shape
    width = pw.shape[1]
    return pl.pallas_call(
        forward_kernel,
        out_shape=(
            jax.ShapeDtypeStruct((positions, width), f32),
            jax.ShapeDtypeStruct((positions, width), bf16),
            jax.ShapeDtypeStruct((positions, channels), bf16),
            jax.ShapeDtypeStruct((channels, positions), bf16),
            jax.ShapeDtypeStruct((2, *tw.shape), bf16),
        ),
        in_specs=[ANY, ANY, ANY, ANY],
        out_specs=(ANY, ANY, VMEM, ANY, ANY),
        scratch_shapes=[
            pltpu.VMEM((positions, width), f32),
            pltpu.VMEM((positions, width), bf16),
            pltpu.VMEM((channels, positions), bf16),
            pltpu.VMEM(feat.shape, bf16),
            pltpu.VMEM(w3.shape, bf16),
            pltpu.VMEM(pw.shape, bf16),
            pltpu.VMEM(tw.shape, bf16),
            pltpu.VMEM(feat.shape, bf16),
            pltpu.VMEM((positions, width), bf16),
            pltpu.VMEM((positions, width), bf16),
            pltpu.VMEM((positions, width), bf16),
            pltpu.VMEM((positions, width), bf16),
            pltpu.VMEM((positions, width), f32),
            pltpu.VMEM((positions, width), bf16),
            pltpu.VMEM(pw.shape, bf16),
            DMA((8,)), DMA((2,)),
            DMA((2,)), DMA((2,)),
            DMA, DMA,
            DMA((4,)), DMA((4,)),
            DMA((3,)), DMA((3,)),
            DMA((4,)), DMA((4,)),
            DMA((2, 3)), DMA((2, 3)),
            DMA((17,)), DMA((17,)),
        ],
        compiler_params=pltpu.CompilerParams(
            collective_id=0, has_side_effects=True, vmem_limit_bytes=67043328
        ),
        name="forward_exchange",
    )(feat, w3, tw, pw)


def backward_kernel(
    feat, hid_hbm, mid_hbm, block_hbm, act_hbm, tw, cot, pw, w3, grad_out, summed,
    hidden, middle, v_feat, block, act_t, v_tw, v_cot, v_pw, v_w3, score, out_grad, slope_f, slope_m,
    hid_grad, mid_grad, later, earlier, swap_out, swap_in, act_out, act_in,
    early, late, sib_early, sib_late, ring_out, ring_in, final, early_out, early_in,
    y_out, y_in, z_tile, z_out, z_in,
    load, tw_load, swap_s, swap_r, acts_s, acts_r, halo_s, halo_r, sibe_s, sibe_r, sibl_s, sibl_r,
    ring_s, ring_r, fin_s, fin_r, y_s, y_r, z_s, z_r,
):
    z, y, c, h, s = place()
    up, down = lax.rem(z + 1, NZ), lax.rem(z + NZ - 1, NZ)
    me = (y * 2 + c) * 2 + s
    corner = c * 2 + s
    channels, tracks = tw.shape
    chunks = channels // COLS
    rows = channels // NZ
    part = rows // NY
    each = part // 4
    sub = rows // HALVES // PIECES
    bf16, f32 = jnp.bfloat16, jnp.float32

    def group(at):
        return {"y": lax.div(at, 4), "c": lax.rem(lax.div(at, 2), 2), "s": lax.rem(at, 2)}

    def corner_of(at):
        return {"c": lax.div(at, 2), "s": lax.rem(at, 2)}

    barrier = pltpu.get_barrier_semaphore()
    greet(barrier, h=1 - h)
    for step in range(1, 16):
        greet(barrier, **group(lax.rem(me + step, 16)))
    for step in range(1, NZ):
        for turn in range(4):
            greet(barrier, z=lax.rem(z + step, NZ), **corner_of(turn))
    greeted = 1 + 15 + 4 * (NZ - 1) + greet_halo(barrier, z, y)

    loads = [
        pltpu.make_async_copy(source, target, load.at[slot])
        for slot, (source, target) in enumerate(
            ((block_hbm, block), (cot, v_cot), (feat, v_feat), (pw, v_pw), (act_hbm, act_t), (w3, v_w3), (hid_hbm, hidden), (mid_hbm, middle))
        )
    ]
    whole, tail = tracks // COLS, tracks % COLS

    def tw_copy(at, size=COLS):
        where = cols_at(at * COLS, size)
        return pltpu.make_async_copy(tw.at[:, where], v_tw.at[:, where], tw_load.at[at])

    loads[0].start()
    loads[1].start()
    repeat(whole, lambda at: tw_copy(at).start())
    tw_copy(whole, tail).start()
    loads[0].wait()
    loads[1].wait()

    def score_step(at, size=COLS):
        tw_copy(at, size).wait()
        cols = cols_at(at * COLS, size)
        value = jax.nn.sigmoid(times(block[...], v_tw[:, cols]))
        score[:, cols] = (v_cot[:, cols].astype(f32) * value).astype(bf16)

    repeat(whole, score_step)
    score_step(whole, tail)
    for copy in loads[2:]:
        copy.start()
    pl.semaphore_wait(barrier, greeted)

    def swap_copy(at):
        return remote(swap_out.at[at], swap_in.at[at], swap_s.at[at], swap_r.at[at], h=1 - h)

    def swap_step(at):
        swap_out[at] = times_transposed(score[...], v_tw[rows_at(at * COLS, COLS), :]).astype(bf16)
        swap_copy(at).start()

    repeat(chunks, swap_step)
    for slot in (2, 3, 6, 7):
        loads[slot].wait()
    slope_m[...] = gelu_slope(middle[...])
    hid_grad[...] = jnp.zeros_like(hid_grad)

    def slope_step(at):
        cols = cols_at(at * COLS, COLS)
        slope_f[at] = gelu_slope(v_feat[:, cols].astype(f32))

    repeat(chunks, slope_step)

    def gather_step(at):
        swap_copy(at).wait_recv()
        where = rows_at(at * COLS, COLS)
        value = swap_out[at].astype(f32) + swap_in[at].astype(f32)
        out_grad[at] = value
        rounded = value.astype(bf16)
        hid_grad[...] += times(rounded, v_pw[where, :])
        early[0, where, :] = transposed_times(rounded, hidden[...]).astype(bf16)

    repeat(chunks, gather_step)
    mid_grad[...] = (hid_grad[...] * slope_m[...]).astype(bf16)
    ahead, behind = (mid_grad, earlier), (mid_grad, later)
    send_halo(z, y, ahead, behind, halo_s, halo_r)

    loads[4].wait()

    def centre_step(at):
        where = rows_at(at * rows, rows)
        early[1, where, :] = times(act_t[where, :], mid_grad[...]).astype(bf16)

    repeat(NZ, centre_step)
    order = (7, 1, 6, 2, 5, 3, 4, 0)

    def early_sibling(slot):
        where = rows_at(lax.rem(z + order[slot], NZ) * rows, rows)
        return remote(early.at[1 - c, where], sib_early.at[where], sibe_s.at[slot], sibe_r.at[slot], c=1 - c)

    for slot in range(NZ):
        early_sibling(slot).start()

    def partial(at, way, piece):
        where = rows_at(at * rows + (way * PIECES + piece) * sub, sub)
        return early[c, where, :].astype(f32) + sib_early[where, :].astype(f32)

    def ring_copy(step, way, piece):
        return remote(
            ring_out.at[step, way, piece], ring_in.at[step, way, piece],
            ring_s.at[step, way, piece], ring_r.at[step, way, piece], z=up if way == 0 else down,
        )

    def ring_step(step):
        for piece in range(PIECES):
            for way in range(HALVES):
                at = lax.rem(z + NZ - 1 - step, NZ) if way == 0 else lax.rem(z + 1 + step, NZ)
                value = partial(at, way, piece)
                if step:
                    ring_copy(step - 1, way, piece).wait_recv()
                    value = value + ring_in[step - 1, way, piece].astype(f32)
                ring_out[step, way, piece] = value.astype(bf16)
                ring_copy(step, way, piece).start()

    early_sibling(0).wait_recv()
    early_sibling(1).wait_recv()
    ring_step(0)
    for slot in range(2, NZ):
        early_sibling(slot).wait_recv()
    ring_step(1)
    ring_step(2)
    wait_halo(z, y, ahead, behind, halo_s, halo_r)

    def late_sibling(at):
        where = rows_at(at * rows, rows)
        return remote(late.at[1 - c, where], sib_late.at[where], sibl_s.at[at], sibl_r.at[at], c=1 - c)

    def late_step(turn):
        at = lax.rem(z + turn, NZ)
        where = rows_at(at * rows, rows)
        late[0, where, :] = times(act_t[where, :], later[...]).astype(bf16)
        late[1, where, :] = times(act_t[where, :], earlier[...]).astype(bf16)
        late_sibling(at).start()

    def y_copy(at, step):
        return remote(
            y_out.at[at, rows_at(lax.rem(y + step, NY) * part, part)], y_in.at[at, step - 1],
            y_s.at[at, step - 1], y_r.at[at, step - 1], y=lax.rem(y + step, NY),
        )

    def y_step(turn):
        at = lax.rem(z + turn, NZ)
        where = rows_at(at * rows, rows)
        late_sibling(at).wait_recv()
        y_out[at] = (late[c, where, :].astype(f32) + sib_late[where, :].astype(f32)).astype(bf16)
        for step in range(1, NY):
            y_copy(at, step).start()

    def act_copy(at):
        return remote(act_out.at[at], act_in.at[at], acts_s.at[at], acts_r.at[at], h=1 - h)

    def act_step(at):
        where = rows_at(at * COLS, COLS)
        value = times_transposed(later[...], v_w3[0, where, :])
        value = value + times_transposed(mid_grad[...], v_w3[1, where, :])
        value = value + times_transposed(earlier[...], v_w3[2, where, :])
        act_out[at] = value.astype(bf16)
        act_copy(at).start()

    def mixed_step(turn):
        act_step(turn - 1)
        late_step(turn + 1)
        y_step(turn)

    loads[5].wait()
    late_step(1)
    repeat(chunks // 2 + 1, mixed_step, 1)
    ring_step(3)
    repeat(chunks + 1, mixed_step, chunks // 2 + 1)
    ring_step(4)
    late_step(NZ)
    y_step(NZ - 1)
    y_step(NZ)

    def z_copy(turn, at, twist):
        to = lax.rem(corner + twist, 4)
        return remote(
            z_out.at[at, to], z_in.at[z, corner], z_s.at[turn - 1, twist], z_r.at[turn - 1, twist],
            z=at, **corner_of(to),
        )

    def z_sum(turn):
        at = lax.rem(z + turn, NZ)
        where = rows_at(at * rows + y * part, part)
        value = late[c, where, :].astype(f32) + sib_late[where, :].astype(f32)
        for step in range(1, NY):
            y_copy(at, step).wait_recv()
            value = value + y_in[at, step - 1].astype(f32)
        z_tile[...] = value
        for to in range(4):
            z_out[at, to] = z_tile[to * each:(to + 1) * each, :].astype(bf16)
        return at

    def z_step(turn):
        at = z_sum(turn)
        for twist in range(4):
            z_copy(turn, at, twist).start()

    z_step(1)
    z_step(2)
    ring_step(5)
    z_step(3)
    z_step(4)
    ring_step(6)
    z_step(5)
    z_step(6)
    z_step(7)
    z_sum(NZ)
    for twist in range(1, 4):
        z_copy(NZ, z, twist).start()
    z_in[z, corner] = z_out[z, corner]

    for piece in range(PIECES):
        for way in range(HALVES):
            value = partial(z, way, piece)
            ring_copy(NZ - 2, way, piece).wait_recv()
            value = value + ring_in[NZ - 2, way, piece].astype(f32)
            final[(way * PIECES + piece) * sub:(way * PIECES + piece + 1) * sub, :] = value
    for at in range(16):
        early_out[at] = final[at * each:(at + 1) * each, :].astype(bf16)

    def fin_copy(step):
        to = lax.rem(me + step, 16)
        return remote(early_out.at[to], early_in.at[me], fin_s.at[step - 1], fin_r.at[step - 1], **group(to))

    for step in range(1, 16):
        fin_copy(step).start()
    early_in[me] = early_out[me]

    def out_step(at):
        act_copy(at).wait_recv()
        value = act_out[at].astype(f32) + act_in[at].astype(f32)
        grad_out[:, cols_at(at * COLS, COLS)] = (out_grad[at] + value * slope_f[at]).astype(bf16)

    repeat(chunks, out_step)
    for turn in range(1, NZ + 1):
        for twist in range(1 if turn == NZ else 0, 4):
            source = lax.rem(z + 2 * NZ - turn, NZ)
            ref = z_in.at[source, lax.rem(corner + 4 - twist, 4)]
            remote(ref, ref, z_s.at[turn - 1, twist], z_r.at[turn - 1, twist], z=z).wait_recv()
    for core in range(2):
        total = jnp.zeros((each, hidden.shape[1]), f32)
        for turn in range(NZ):
            for sample in range(2):
                total = total + z_in[turn, core * 2 + sample].astype(f32)
        summed[2 + core] = total
    for step in range(1, 16):
        ref = early_in.at[lax.rem(me + 16 - step, 16)]
        remote(ref, ref, fin_s.at[step - 1], fin_r.at[step - 1], z=z).wait_recv()
    for core in range(2):
        total = jnp.zeros((each, hidden.shape[1]), f32)
        for row in range(NY):
            for sample in range(2):
                total = total + early_in[(row * 2 + core) * 2 + sample].astype(f32)
        summed[core] = total

    def drain_chunks(at):
        swap_copy(at).wait_send()
        act_copy(at).wait_send()

    repeat(chunks, drain_chunks)
    drain_halo(z, y, ahead, behind, halo_s, halo_r)
    for slot in range(NZ):
        early_sibling(slot).wait_send()
    for step in range(NZ - 1):
        for piece in range(PIECES):
            for way in range(HALVES):
                ring_copy(step, way, piece).wait_send()

    def drain_late(at):
        late_sibling(at).wait_send()
        for step in range(1, NY):
            y_copy(at, step).wait_send()

    repeat(NZ, drain_late)
    for turn in range(1, NZ + 1):
        for twist in range(1 if turn == NZ else 0, 4):
            z_copy(turn, lax.rem(z + turn, NZ), twist).wait_send()
    for step in range(1, 16):
        fin_copy(step).wait_send()


def backward(feat, hidden, middle, block, act_t, tw, cot, pw, w3):
    bf16, f32 = jnp.bfloat16, jnp.float32
    positions, channels = feat.shape
    width = pw.shape[1]
    tracks = tw.shape[1]
    chunks = channels // COLS
    rows = channels // NZ
    part = rows // NY
    each = part // 4
    sub = rows // HALVES // PIECES
    ring = (NZ - 1, HALVES, PIECES)
    tile = (chunks, positions, COLS)
    return pl.pallas_call(
        backward_kernel,
        out_shape=(
            jax.ShapeDtypeStruct((positions, channels), bf16),
            jax.ShapeDtypeStruct((4, each, width), f32),
        ),
        in_specs=[ANY] * 9,
        out_specs=(VMEM, VMEM),
        scratch_shapes=[
            pltpu.VMEM(hidden.shape, bf16),
            pltpu.VMEM(middle.shape, f32),
            pltpu.VMEM(feat.shape, bf16),
            pltpu.VMEM(feat.shape, bf16),
            pltpu.VMEM(act_t.shape, bf16),
            pltpu.VMEM(tw.shape, bf16),
            pltpu.VMEM(cot.shape, bf16),
            pltpu.VMEM(pw.shape, bf16),
            pltpu.VMEM(w3.shape, bf16),
            pltpu.VMEM((positions, tracks), bf16),
            pltpu.VMEM(tile, f32),
            pltpu.VMEM(tile, f32),
            pltpu.VMEM((positions, width), f32),
            pltpu.VMEM((positions, width), f32),
            pltpu.VMEM((positions, width), bf16),
            pltpu.VMEM((positions, width), bf16),
            pltpu.VMEM((positions, width), bf16),
            pltpu.VMEM(tile, bf16),
            pltpu.VMEM(tile, bf16),
            pltpu.VMEM(tile, bf16),
            pltpu.VMEM(tile, bf16),
            pltpu.VMEM((2, channels, width), bf16),
            pltpu.VMEM((2, channels, width), bf16),
            pltpu.VMEM((channels, width), bf16),
            pltpu.VMEM((channels, width), bf16),
            pltpu.VMEM((*ring, sub, width), bf16),
            pltpu.VMEM((*ring, sub, width), bf16),
            pltpu.VMEM((rows, width), f32),
            pltpu.VMEM((16, each, width), bf16),
            pltpu.VMEM((16, each, width), bf16),
            pltpu.VMEM((NZ, rows, width), bf16),
            pltpu.VMEM((NZ, NY - 1, part, width), bf16),
            pltpu.VMEM((part, width), f32),
            pltpu.VMEM((NZ, 4, each, width), bf16),
            pltpu.VMEM((NZ, 4, each, width), bf16),
            DMA((8,)), DMA((tracks // COLS + 1,)),
            DMA((chunks,)), DMA((chunks,)),
            DMA((chunks,)), DMA((chunks,)),
            DMA((2,)), DMA((2,)),
            DMA((NZ,)), DMA((NZ,)),
            DMA((NZ,)), DMA((NZ,)),
            DMA(ring), DMA(ring),
            DMA((15,)), DMA((15,)),
            DMA((NZ, NY - 1)), DMA((NZ, NY - 1)),
            DMA((NZ, 4)), DMA((NZ, 4)),
        ],
        compiler_params=pltpu.CompilerParams(
            collective_id=1, has_side_effects=True, vmem_limit_bytes=60000000
        ),
        name="backward",
    )(feat, hidden, middle, block, act_t, tw, cot, pw, w3)


def body(features, dilated_weight, point_weight, track_weight, track_cotangent):
    samples, positions, channels = features.shape
    number_rows = samples * positions
    feat = features.reshape(number_rows, channels)
    taps_weight = jnp.transpose(dilated_weight, (1, 0, 2))
    middle, hidden, block, turned, whole_track = forward_exchange(
        feat, taps_weight, track_weight, point_weight
    )
    whole_track = whole_track.reshape(channels, track_weight.shape[1])
    cotangent = track_cotangent.reshape(number_rows, whole_track.shape[1])
    input_grad, summed = backward(
        feat, hidden, middle, block, turned, whole_track, cotangent, point_weight, taps_weight
    )
    dilated_grad = jnp.stack([summed[2], summed[1], summed[3]], axis=1)
    return (input_grad.reshape(samples, positions, channels), dilated_grad, summed[0])


def solution(mesh):
    torus = Mesh(
        mesh.devices.reshape(NZ, NY, 2, mesh.shape["head"], mesh.shape["sample"]),
        ("z", "y", "c", "h", "s"),
    )
    placed = (
        P("s", SEQ, None),
        P(None, None, "h"),
        P(None, "h"),
        P("s", "h"),
        P("s", SEQ, "h"),
    )
    return jax.shard_map(
        body,
        mesh=torus,
        in_specs=placed,
        out_specs=(P("s", SEQ, None), P(SEQ_SAMPLE, None, "h"), P(SEQ_SAMPLE, "h")),
        check_vma=False,
    )
```
